256 devices in a mesh: slab: 16 (over z_lo, y), front: 16 (over x, z_hi, core).
Axes of the slice: x: 4, y: 4, z: 8 (z_hi: 2, z_lo: 4; z = z_hi * 4 + z_lo), core: 2. Of those that a mesh axis runs over, the one named last changes fastest.
Arguments:
- sources: float32 [2, 16, 16384, 128], P(None, 'slab', 'front'), may hold values from -6 to 6
- front_inv: float32 [16, 16384, 512], P('slab', 'front'), may hold values from -0.25 to 0.25
- pattern: int32 [16, 256, 4], P('slab', 'front'), may hold values from 0 to 15, all different within a row
- tree: int32 [16, 16, 4], P('slab', 'front'), may hold values from 0 to 15, all different within a row
- lift: float32 [16, 8192, 256], P('slab', 'front'), may hold values from -0.1875 to 0.1875
- spread: float32 [16, 2048, 1024], P('slab', 'front'), may hold values from -0.1875 to 0.1875
- couple: float32 [16, 2048, 256], P('slab', 'front'), may hold values from -0.375 to 0.375
- sep_inv: float32 [16, 2048, 4096], P('slab', 'front'), may hold values from -0.09375 to 0.09375
- inflow: float32 [16, 2048, 128], P('slab', 'front'), may hold values from -6 to 6
Outputs:
- leaf_field: float32 [2, 16, 16384, 128], P(None, 'slab', 'front')
The draws below stay inside these ranges and needn't reach their ends.
Inputs may be any that keep to these rules, and one draw needn't show every extreme that they name: `pattern`: each block row names 4 different block columns. `tree`: each leaf names 4 different separator blocks.
All inputs are finite; a program needn't handle non-finite values.
Results may differ from the reference program's by a relative error of at most 0.0001.
Values sent between devices are 32-bit elements; how exact they have to be, the bound alone decides.
No kernel may reach another device: no remote copies, remote signals or barrier semaphores. Data moves between devices by JAX's collectives and lax.ppermute only.
A program may use at most 128 MiB of HBM per device.

```python
import jax
import jax.numpy as jnp
from jax import lax

NRHS = 64
BEATS = 2
LEAF = 1024
SEP = 2048
BLK = 64
NB = 4
BND = 128
P_SIZE = 4
LEAVES = 16
BROWS = 16
SBL = 16
N_SLAB = 16


def steps_of(own_key, extent, cuts, smallest, high):
    factor_of, own = 1.0, jax.random.fold_in(own_key, 6)
    for position, shards_of in cuts:
        draws = jnp.exp(jax.random.uniform(jax.random.fold_in(own, position), (shards_of,), jnp.float32, smallest / len(cuts), high / len(cuts)))
        factor_of = factor_of * jnp.repeat(draws, extent[position] // shards_of).reshape([-1 if axis == position else 1 for axis in range(len(extent))])
    return factor_of


def choose_distinct(own_key, rows, number_of, top, lift):
    sequence = jax.random.permutation(jax.random.fold_in(own_key, 1), number_of)
    favour = sequence
    for power in range(3):
        favour = favour * favour // number_of
    favour = favour * lift // number_of
    chance = jax.random.randint(jax.random.fold_in(own_key, 2), (rows, number_of), 0, 4096) + favour
    holders = jax.random.permutation(jax.random.fold_in(own_key, 3), rows)[jnp.arange(number_of) % rows]
    chance = jnp.where(jnp.arange(rows)[:, None] == holders[None, :], 1 << 14, chance)
    priority = chance * number_of + jnp.arange(number_of)
    return lax.top_k(priority.astype(jnp.int32), top)[1].astype(jnp.int32)


def scatter_about(stream_key, extent, deviation, most, shards=(), kind=jnp.bfloat16):
    loudness = steps_of(stream_key, extent, shards, -0.22, 0.18) if shards else 1.0
    values = jax.random.normal(stream_key, extent, jnp.float32) * deviation * loudness
    return jnp.minimum(jnp.maximum(values, -most), most).astype(kind)


def setup_inputs(seed: int = 0) -> dict:
    splits = jax.random.split(jax.random.key(seed), 10)
    return {
        "sources": scatter_about(splits[0], (BEATS, N_SLAB, LEAVES * LEAF, 2 * NRHS), 1.0, 6.0, ((1, 16), (2, 16)), jnp.float32),
        "front_inv": scatter_about(splits[1], (N_SLAB, LEAVES * LEAF, NB * 2 * BLK), (NB * 2 * BLK) ** -0.5, 0.25, ((0, 16), (1, 16)), jnp.float32),
        "pattern": choose_distinct(splits[2], N_SLAB * (LEAVES * BROWS), BROWS, NB, 0).reshape((N_SLAB, LEAVES * BROWS, NB)),
        "tree": choose_distinct(splits[3], N_SLAB * LEAVES, SBL, P_SIZE, 0).reshape((N_SLAB, LEAVES, P_SIZE)),
        "lift": scatter_about(splits[4], (N_SLAB, LEAVES * P_SIZE * BND, 2 * BND), (2 * P_SIZE * BND) ** -0.5, 0.1875, ((0, 16), (1, 16)), jnp.float32),
        "spread": scatter_about(splits[5], (N_SLAB, LEAVES * BND, P_SIZE * 2 * BND), (2 * P_SIZE * BND) ** -0.5, 0.1875, ((0, 16), (1, 16)), jnp.float32),
        "couple": scatter_about(splits[6], (N_SLAB, LEAVES * BND, 2 * BND), (2 * BND) ** -0.5, 0.375, ((0, 16), (1, 16)), jnp.float32),
        "sep_inv": scatter_about(splits[7], (N_SLAB, SEP, 2 * SEP), (2 * SEP) ** -0.5, 0.09375, ((0, 16), (1, 16)), jnp.float32),
        "inflow": scatter_about(splits[8], (N_SLAB, LEAVES * BND, 2 * NRHS), 1.0, 6.0, ((0, 16), (1, 16)), jnp.float32),
    }


HIGH = lax.Precision.HIGHEST


def twist(field):
    half = field.shape[-1] // 2
    return jnp.concatenate([-field[..., half:], field[..., :half]], axis=-1)


def paired(field):
    return jnp.concatenate([field, twist(field)], axis=-2)


def packed(matrix, field):
    return jnp.einsum("ik,kc->ic", matrix, paired(field), precision=HIGH)


def front_apply(g_rows, patt, field):
    cols = field.shape[-1]
    blocks = field.reshape(LEAF // BLK, BLK, cols)
    picked = jnp.take(blocks, patt, axis=0)
    both = jnp.stack([picked, twist(picked)], axis=2).reshape(LEAF // BLK, NB * 2 * BLK, cols)
    matrix = g_rows.reshape(LEAF // BLK, BLK, NB * 2 * BLK)
    return jnp.einsum("rik,rkc->ric", matrix, both, precision=HIGH).reshape(LEAF, cols)


def leaf_map(fn):
    return jax.vmap(jax.vmap(fn))


def reference(sources, front_inv, pattern, tree, lift, spread, couple, sep_inv, inflow):
    cols = sources.shape[-1]
    sbl = SEP // BND
    gmat = front_inv.reshape(N_SLAB, LEAVES, LEAF, NB * 2 * BLK)
    patt = pattern.reshape(N_SLAB, LEAVES, LEAF // BLK, NB)
    cmat = lift.reshape(N_SLAB, LEAVES, P_SIZE * BND, 2 * BND)
    bmat = spread.reshape(N_SLAB, LEAVES, BND, P_SIZE * 2 * BND)
    kmat = couple.reshape(N_SLAB, LEAVES, BND, 2 * BND)
    select = (tree[..., None] == jnp.arange(sbl, dtype=jnp.int32)).astype(jnp.float32)
    wave = inflow.reshape(N_SLAB, LEAVES, BND, cols)
    results = []
    outgoing = wave
    for beat in range(BEATS):
        forcing = sources[beat].reshape(N_SLAB, LEAVES, LEAF, cols)
        ylocal = leaf_map(front_apply)(gmat, patt, forcing)
        if beat == 0:
            incoming = wave
        else:
            incoming = jnp.concatenate([jnp.zeros_like(outgoing[:1]), outgoing[:-1]], axis=0)
        drive = leaf_map(packed)(kmat, incoming) - ylocal[:, :, LEAF - BND:, :]
        contrib = leaf_map(packed)(cmat, drive).reshape(N_SLAB, LEAVES, P_SIZE, BND, cols)
        rhs = jnp.einsum("slpb,slpic->sbic", select, contrib, precision=HIGH).reshape(N_SLAB, SEP, cols)
        sol = jax.vmap(packed)(sep_inv, rhs).reshape(N_SLAB, sbl, BND, cols)
        picked = jnp.einsum("slpb,sbic->slpic", select, sol, precision=HIGH)
        stacked = jnp.stack([picked, twist(picked)], axis=3).reshape(N_SLAB, LEAVES, P_SIZE * 2 * BND, cols)
        zvals = jnp.einsum("slik,slkc->slic", bmat, stacked, precision=HIGH)
        embed = jnp.concatenate([jnp.zeros((N_SLAB, LEAVES, LEAF - BND, cols), jnp.float32), zvals], axis=2)
        solved = ylocal - leaf_map(front_apply)(gmat, patt, embed)
        results.append(solved.reshape(N_SLAB, LEAVES * LEAF, cols))
        outgoing = solved[:, :, LEAF - BND:, :]
    return jnp.stack(results)
```

```python
import functools

import jax
import jax.numpy as jnp
from jax import lax
from jax.experimental import pallas as pl
from jax.experimental.pallas import tpu as pltpu
from jax.sharding import Mesh
from jax.sharding import PartitionSpec as P

BEATS = 2
LEAF = 1024
SEP = 2048
BLK = 64
NB = 4
BND = 128
P_SIZE = 4
BROWS = LEAF // BLK
FRONT = ("front_0", "front_1", "front_2")
X, Z, C = FRONT
NX = 4
HALF = SEP // 2
QUARTER = HALF // NX
F32 = jnp.float32
BF16 = jnp.bfloat16


def twist(field):
    half = field.shape[-1] // 2
    lane = lax.broadcasted_iota(jnp.int32, field.shape, len(field.shape) - 1)
    turned = pltpu.roll(field, half, len(field.shape) - 1)
    return jnp.where(lane < half, -turned, turned)


def split(a):
    high = a.astype(BF16)
    low = (a - high.astype(F32)).astype(BF16)
    return high, low


def mm(a, b):
    return jnp.dot(a, b, preferred_element_type=F32)


def rows_split(a):
    return jnp.concatenate(split(a), axis=0)


def cols_split(b):
    return jnp.concatenate(split(b), axis=1)


def product(stacked, paired):
    rows, cols = stacked.shape[0] // 2, paired.shape[1] // 2
    full = mm(stacked, paired)
    return full[:rows, :cols] + (full[:rows, cols:] + full[rows:, :cols])


def product3(a, b):
    ah, al = split(a)
    bh, bl = split(b)
    return mm(ah, bh) + (mm(ah, bl) + mm(al, bh))


def packed(matrix, field):
    both = jnp.concatenate([field, twist(field)], axis=0)
    return product(rows_split(matrix), cols_split(both))


def front_rows(g, patt_ref, row, take):
    both = []
    for k in range(NB):
        block = take(patt_ref[row, k])
        both.append(block[0])
        both.append(block[1])
    return product3(g, jnp.concatenate(both, axis=0))


def tail_columns(g, patt_ref, row):
    parts = []
    for block in (BROWS - 2, BROWS - 1):
        total = jnp.zeros((BLK, 2 * BLK), F32)
        for k in range(NB):
            held = (patt_ref[row, k] == block).astype(F32)
            total = total + held * g[:, k * 2 * BLK : (k + 1) * 2 * BLK]
        parts.append(total)
    return jnp.concatenate(parts, axis=1)


def tail_field(z):
    tz = twist(z)
    return jnp.concatenate([z[:BLK], tz[:BLK], z[BLK:], tz[BLK:]], axis=0)


def start_kernel(patt_ref, src_ref, g_ref, couple_ref, wave_ref, y_ref, drive_ref):
    def take(block):
        at = pl.ds(pl.multiple_of(block * BLK, BLK), BLK)
        a, b = src_ref[0, at, :], src_ref[1, at, :]
        return (
            jnp.concatenate([a, b], axis=1),
            jnp.concatenate([twist(a), twist(b)], axis=1),
        )

    for i in range(2):
        at = slice(i * BLK, (i + 1) * BLK)
        y = front_rows(g_ref[at, :], patt_ref, BROWS - 2 + i, take)
        y_ref[0, at, :] = y[:, :BND]
        y_ref[1, at, :] = y[:, BND:]
    drive_ref[...] = packed(couple_ref[...], wave_ref[...]) - y_ref[0]


def drive_kernel(couple_ref, wave_ref, y_ref, drive_ref):
    drive_ref[...] = packed(couple_ref[...], wave_ref[...]) - y_ref[0]


def lift_kernel(own_tree, far_tree, own_ref, far_ref, own_lift, far_lift, o0, o1, o2, o3, acc):
    x, c = lax.axis_index(X), lax.axis_index(C)
    acc[...] = jnp.zeros_like(acc)
    for tree, drive_ref, mat in ((own_tree, own_ref, own_lift), (far_tree, far_ref, far_lift)):
        drive = drive_ref[...]
        pair = cols_split(jnp.concatenate([drive, twist(drive)], axis=0))
        for p in range(P_SIZE):
            block = tree[p]

            @pl.when(block // 8 == c)
            def _():
                owner = (block % 8) // 2
                slot = lax.rem(owner - x + NX, NX) * 2 + block % 2
                acc[slot] += product(rows_split(mat[p * BND : (p + 1) * BND, :]), pair)

    for d, out in enumerate((o0, o1, o2, o3)):
        out[:BND] = acc[2 * d]
        out[BND:] = acc[2 * d + 1]


def sep_kernel(r0, r1, r2, r3, own_ref, far_ref, own_out, far_out):
    x, c = lax.axis_index(X), lax.axis_index(C)
    total = None
    for d, r in enumerate((r0, r1, r2, r3)):
        col = c * HALF + lax.rem(x - d + NX, NX) * QUARTER
        real = pl.ds(pl.multiple_of(col, QUARTER), QUARTER)
        imag = pl.ds(pl.multiple_of(SEP + col, QUARTER), QUARTER)
        rows = jnp.concatenate(
            [own_ref[:, real], own_ref[:, imag], far_ref[:, real], far_ref[:, imag]], axis=0
        )
        part = product(rows_split(rows), cols_split(r[...]))
        total = part if total is None else total + part
    own_out[...] = total[:BND] + twist(total[BND : 2 * BND])
    far_out[...] = total[2 * BND : 3 * BND] + twist(total[3 * BND :])


def spread_kernel(own_tree, far_tree, q0, q1, q2, q3, own_mat, far_mat, own_out, far_out, sol):
    x, z, c = lax.axis_index(X), lax.axis_index(Z), lax.axis_index(C)
    for d, q in enumerate((q0, q1, q2, q3)):
        sol[2 * d] = q[:BND]
        sol[2 * d + 1] = q[BND:]
    for tree, mat, out in ((own_tree, own_mat, own_out), (far_tree, far_mat, far_out)):
        out[...] = jnp.zeros_like(out)
        for p in range(P_SIZE):
            block = tree[p]

            @pl.when(block % 2 == c)
            def _():
                side = lax.rem((block // 2) % 2 + z, 2)
                slot = lax.rem(x - block // 4 + NX, NX) * 2 + side
                out[...] += packed(mat[:, p * 2 * BND : (p + 1) * 2 * BND], sol[slot])


def out_kernel(patt_ref, near_ref, far_ref, y_ref, g_ref, z_ref, out_ref):
    z = near_ref[...] + far_ref[...]
    z_ref[...] = z
    tail = cols_split(tail_field(z))
    for i in range(2):
        at = slice(i * BLK, (i + 1) * BLK)
        cols = tail_columns(g_ref[at, :], patt_ref, BROWS - 2 + i)
        out_ref[at, :] = y_ref[0, at, :] - product(rows_split(cols), tail)


STEP_ROWS = 256


def bulk_kernel(patt_ref, src_ref, z_ref, g_ref, out_ref, field):
    @pl.when(pl.program_id(0) == 0)
    def _():
        for b in range(BROWS):
            at = slice(b * BLK, (b + 1) * BLK)
            first = src_ref[0, at, :]
            if b >= BROWS - 2:
                first = first - z_ref[(b - BROWS + 2) * BLK : (b - BROWS + 3) * BLK, :]
            second = src_ref[1, at, :]
            field[b, 0] = jnp.concatenate([first, second], axis=1)
            field[b, 1] = jnp.concatenate([twist(first), twist(second)], axis=1)

    def take(block):
        return field[block, 0], field[block, 1]

    for i in range(STEP_ROWS // BLK):
        at = slice(i * BLK, (i + 1) * BLK)
        row = pl.program_id(0) * (STEP_ROWS // BLK) + i
        y = front_rows(g_ref[at, :], patt_ref, row, take)
        out_ref[0, at, :] = y[:, :BND]
        out_ref[1, at, :] = y[:, BND:]


def last_kernel(patt_ref, near_ref, far_ref, g_ref, y_ref, out_ref):
    tail = cols_split(tail_field(near_ref[...] + far_ref[...]))
    cols = jnp.concatenate(
        [
            tail_columns(
                g_ref[i * BLK : (i + 1) * BLK, :],
                patt_ref,
                pl.program_id(0) * (STEP_ROWS // BLK) + i,
            )
            for i in range(STEP_ROWS // BLK)
        ],
        axis=0,
    )
    out_ref[0] = y_ref[0] - product(rows_split(cols), tail)


VM = pl.BlockSpec(memory_space=pltpu.VMEM)
SM = pl.BlockSpec(memory_space=pltpu.SMEM)


def shape(*dims):
    return jax.ShapeDtypeStruct(dims, F32)


ROOM = pltpu.CompilerParams(vmem_limit_bytes=12 << 20)


def cost(flops, size):
    return pl.CostEstimate(flops=flops, bytes_accessed=size, transcendentals=0)


def shifted(value, axis, distance):
    size = lax.axis_size(axis)
    return lax.ppermute(value, axis, [(i, (i + distance) % size) for i in range(size)])


def swapped(value, axis):
    return shifted(value, axis, 1)


def on_device(sources, front_inv, pattern, tree, lift, spread, couple, sep_inv, inflow):
    src = sources[:, 0]
    gmat, patt, own_tree = front_inv[0], pattern[0], tree[0, 0]
    own_lift, own_spread, kmat, own_sep, wave = lift[0], spread[0], couple[0], sep_inv[0], inflow[0]
    steps = LEAF // STEP_ROWS
    whole = lambda *dims: pl.BlockSpec(dims, lambda *i: (0,) * len(dims))
    tail_g = pl.BlockSpec((BND, NB * 2 * BLK), lambda i: (LEAF // BND - 1, 0))

    far_tree = swapped(own_tree, C)
    far_lift = swapped(own_lift, C)
    far_sep = swapped(own_sep, C)
    far_spread = swapped(own_spread, C)

    ytail, drive = pl.pallas_call(
        start_kernel,
        grid=(1,),
        in_specs=[SM, whole(2, LEAF, BND), tail_g, whole(BND, 2 * BND), whole(BND, BND)],
        out_specs=[whole(2, BND, BND), whole(BND, BND)],
        out_shape=[shape(2, BND, BND), shape(BND, BND)],
        compiler_params=ROOM,
        cost_estimate=cost(2 * 128 * 512 * 256 * 6, 1 << 21),
        name="start",
    )(patt, src, gmat, kmat, wave)

    def tail_of(beat):
        return pl.BlockSpec((1, BND, BND), lambda i, beat=beat: (beat, 0, 0))

    result = None
    for beat in range(BEATS):
        if beat:
            devices = lax.axis_size("slab")
            incoming = lax.ppermute(outgoing, "slab", [(i, i + 1) for i in range(devices - 1)])
            drive = pl.pallas_call(
                drive_kernel,
                grid=(1,),
                in_specs=[whole(BND, 2 * BND), whole(BND, BND), tail_of(beat)],
                out_specs=whole(BND, BND),
                out_shape=shape(BND, BND),
                compiler_params=ROOM,
            cost_estimate=cost(2 * 128 * 256 * 128 * 4, 1 << 18),
                name=f"drive{beat}",
            )(kmat, incoming, ytail)
        far_drive = swapped(drive, C)
        pieces = pl.pallas_call(
            lift_kernel,
            in_specs=[SM, SM, VM, VM, VM, VM],
            out_specs=[VM] * NX,
            out_shape=[shape(2 * BND, BND)] * NX,
            scratch_shapes=[pltpu.VMEM((2 * NX, BND, BND), F32)],
            compiler_params=ROOM,
            cost_estimate=cost(2 * 512 * 256 * 128 * 4, 3 << 19),
            name=f"lift{beat}",
        )(own_tree, far_tree, drive, far_drive, own_lift, far_lift)
        came = [shifted(pieces[d], X, d) for d in range(1, NX)]
        near = (pieces[0] + came[0]) + (came[1] + came[2])
        mine = near + swapped(near, Z)
        held = [mine] + [shifted(mine, X, d) for d in range(1, NX)]
        own_part, far_part = pl.pallas_call(
            sep_kernel,
            in_specs=[VM] * 6,
            out_specs=[VM] * 2,
            out_shape=[shape(BND, BND)] * 2,
            compiler_params=ROOM,
            cost_estimate=cost(2 * 256 * 2048 * 128 * 4, 5 << 20),
            name=f"sep{beat}",
        )(*held, own_sep, far_sep)
        sol = own_part + swapped(far_part, C)
        pair = jnp.concatenate([sol, swapped(sol, Z)], axis=0)
        held = [pair] + [shifted(pair, X, d) for d in range(1, NX)]
        own_z, far_z = pl.pallas_call(
            spread_kernel,
            in_specs=[SM, SM] + [VM] * 6,
            out_specs=[VM] * 2,
            out_shape=[shape(BND, BND)] * 2,
            scratch_shapes=[pltpu.VMEM((2 * NX, BND, BND), F32)],
            compiler_params=ROOM,
            cost_estimate=cost(2 * 128 * 1024 * 128 * 4, 3 << 19),
            name=f"spread{beat}",
        )(own_tree, far_tree, *held, own_spread, far_spread)
        came = swapped(far_z, C)
        if beat == 0:
            zvals, outgoing = pl.pallas_call(
                out_kernel,
                grid=(1,),
                in_specs=[SM, whole(BND, BND), whole(BND, BND), tail_of(0), tail_g],
                out_specs=[whole(BND, BND)] * 2,
                out_shape=[shape(BND, BND)] * 2,
                compiler_params=ROOM,
            cost_estimate=cost(2 * 128 * 256 * 128 * 4, 1 << 19),
                name="outgoing",
            )(patt, own_z, came, ytail, gmat)
            result = pl.pallas_call(
                bulk_kernel,
                grid=(steps,),
                in_specs=[
                    SM,
                    whole(2, LEAF, BND),
                    whole(BND, BND),
                    pl.BlockSpec((STEP_ROWS, NB * 2 * BLK), lambda i: (i, 0)),
                ],
                out_specs=pl.BlockSpec((2, STEP_ROWS, BND), lambda i: (0, i, 0)),
                out_shape=shape(2, LEAF, BND),
                scratch_shapes=[pltpu.VMEM((BROWS, 2, BLK, 2 * BND), F32)],
                compiler_params=ROOM,
            cost_estimate=cost(2 * 1024 * 512 * 256 * 6, 4 << 20),
                name="bulk",
            )(patt, src, zvals, gmat)
        else:
            second = pl.BlockSpec((1, STEP_ROWS, BND), lambda i: (1, i, 0))
            result = pl.pallas_call(
                last_kernel,
                grid=(steps,),
                in_specs=[
                    SM,
                    whole(BND, BND),
                    whole(BND, BND),
                    pl.BlockSpec((STEP_ROWS, NB * 2 * BLK), lambda i: (i, 0)),
                    second,
                ],
                out_specs=second,
                out_shape=shape(2, LEAF, BND),
                input_output_aliases={4: 0},
                compiler_params=ROOM,
            cost_estimate=cost(2 * 1024 * 256 * 128 * 4, 3 << 20),
                name="last",
            )(patt, own_z, came, gmat, result)
    return result[:, None]


def solution(mesh):
    torus = Mesh(
        mesh.devices.reshape(mesh.shape["slab"], 4, 2, 2), ("slab", "front_0", "front_1", "front_2")
    )
    in_specs = (
        P(None, "slab", FRONT, None),
        P("slab", FRONT, None),
        P("slab", FRONT, None),
        P("slab", FRONT, None),
        P("slab", FRONT, None),
        P("slab", FRONT, None),
        P("slab", FRONT, None),
        P("slab", FRONT, None),
        P("slab", FRONT, None),
    )
    out_specs = P(None, "slab", FRONT, None)
    return jax.shard_map(
        on_device, mesh=torus, in_specs=in_specs, out_specs=out_specs, check_vma=False
    )
```

```python
import functools

import jax
import jax.numpy as jnp
from jax import lax
from jax.experimental import pallas as pl
from jax.experimental.pallas import tpu as pltpu
from jax.sharding import Mesh
from jax.sharding import PartitionSpec as P

BEATS = 2
LEAF = 1024
SEP = 2048
BLK = 64
NB = 4
BND = 128
P_SIZE = 4
BROWS = LEAF // BLK
FRONT = ("front_0", "front_1", "front_2")
X, Z, C = FRONT
NX = 4
HALF = SEP // 2
QUARTER = HALF // NX
F32 = jnp.float32
BF16 = jnp.bfloat16


def twist(field):
    half = field.shape[-1] // 2
    lane = lax.broadcasted_iota(jnp.int32, field.shape, len(field.shape) - 1)
    turned = pltpu.roll(field, half, len(field.shape) - 1)
    return jnp.where(lane < half, -turned, turned)


def split(a):
    high = a.astype(BF16)
    low = (a - high.astype(F32)).astype(BF16)
    return high, low


def mm(a, b):
    return jnp.dot(a, b, preferred_element_type=F32)


def rows_split(a):
    return jnp.concatenate(split(a), axis=0)


def cols_split(b):
    return jnp.concatenate(split(b), axis=1)


def product(stacked, paired):
    rows, cols = stacked.shape[0] // 2, paired.shape[1] // 2
    full = mm(stacked, paired)
    return full[:rows, :cols] + (full[:rows, cols:] + full[rows:, :cols])


def packed(matrix, field):
    both = jnp.concatenate([field, twist(field)], axis=0)
    return product(rows_split(matrix), cols_split(both))


def front_rows(g, field):
    gh, gl = split(g)
    fh, fl = split(field)
    rows = g.shape[0]
    first = mm(jnp.concatenate([gh, gl], axis=0), fh)
    return first[:rows] + (first[rows:] + mm(gh, fl))


def gathered(patt_ref, row, take):
    both = []
    for k in range(NB):
        a, b = take(patt_ref[k, row])
        both.append(jnp.concatenate([a, b], axis=1))
        both.append(jnp.concatenate([twist(a), twist(b)], axis=1))
    return jnp.concatenate(both, axis=0)


def tail_columns(g, patt_ref, row):
    parts = []
    for block in (BROWS - 2, BROWS - 1):
        total = jnp.zeros((BLK, 2 * BLK), F32)
        for k in range(NB):
            held = (patt_ref[k, row] == block).astype(F32)
            total = total + held * g[:, k * 2 * BLK : (k + 1) * 2 * BLK]
        parts.append(total)
    return jnp.concatenate(parts, axis=1)


def tail_field(z):
    tz = twist(z)
    return jnp.concatenate([z[:BLK], tz[:BLK], z[BLK:], tz[BLK:]], axis=0)


def start_kernel(
    patt_ref, src_ref, g_ref, couple_ref, wave_ref, y_ref, drive_ref, g_out, blocks, held, couple, wave, sems
):
    copies = [
        pltpu.make_async_copy(g_ref.at[0, pl.ds(LEAF - BND, BND), :], held, sems.at[0]),
        pltpu.make_async_copy(couple_ref.at[0], couple, sems.at[1]),
        pltpu.make_async_copy(wave_ref.at[0], wave, sems.at[2]),
    ]
    for i in range(2):
        for k in range(NB):
            at = pl.ds(pl.multiple_of(patt_ref[k, BROWS - 2 + i] * BLK, BLK), BLK)
            n = i * NB + k
            copies.append(
                pltpu.make_async_copy(src_ref.at[:, 0, at, :], blocks.at[n], sems.at[3 + n])
            )
    for copy in copies:
        copy.start()
    for copy in copies:
        copy.wait()
    g_out[...] = held[...]
    for i in range(2):
        at = slice(i * BLK, (i + 1) * BLK)
        both = []
        for k in range(NB):
            pair = blocks[i * NB + k]
            both.append(jnp.concatenate([pair[0], pair[1]], axis=1))
            both.append(jnp.concatenate([twist(pair[0]), twist(pair[1])], axis=1))
        y = front_rows(held[at, :], jnp.concatenate(both, axis=0))
        y_ref[0, at, :] = y[:, :BND]
        y_ref[1, at, :] = y[:, BND:]
    drive_ref[...] = packed(couple[...], wave[...]) - y_ref[0]


def drive_kernel(couple_ref, wave_ref, y_ref, drive_ref):
    drive_ref[...] = packed(couple_ref[...], wave_ref[...]) - y_ref[0]


def owner_slot(distance, c):
    return jnp.where(distance == 1, 1 + c, jnp.where(distance == 3, 2 - c, (distance // 2) * 3))


def slot_distance(slot, c):
    return (0, 1 + 2 * c, 3 - 2 * c, 2)[slot]


def lift_kernel(own_tree, far_tree, own_ref, far_ref, own_lift, far_lift, *refs):
    outs, acc = refs[:-1], refs[-1]
    x, c = lax.axis_index(X), lax.axis_index(C)
    acc[...] = jnp.zeros_like(acc)
    parts = []
    for drive_ref, mat in ((own_ref, own_lift), (far_ref, far_lift)):
        drive = drive_ref[...]
        pair = cols_split(jnp.concatenate([drive, twist(drive)], axis=0))
        parts.append(product(rows_split(mat[...]), pair))
    for tree, part in zip((own_tree, far_tree), parts):
        for p in range(P_SIZE):
            block = tree[p]

            @pl.when(block // 8 == c)
            def _():
                owner = (block % 8) // 2
                slot = owner_slot(jnp.bitwise_xor(owner, x), c) * 2 + block % 2
                acc[slot] += part[p * BND : (p + 1) * BND]

    for i, out in enumerate(outs):
        out[:BND] = acc[2 * i]
        out[BND:] = acc[2 * i + 1]


def sep_kernel(*refs):
    pieces, (own_ref, far_ref, own_out, far_out) = refs[:-4], refs[-4:]
    x, c = lax.axis_index(X), lax.axis_index(C)
    total = None
    for slot, piece in enumerate(pieces):
        owner = jnp.bitwise_xor(x, slot_distance(slot, c))
        col = c * HALF + owner * QUARTER
        real = pl.ds(pl.multiple_of(col, QUARTER), QUARTER)
        imag = pl.ds(pl.multiple_of(SEP + col, QUARTER), QUARTER)
        rows = jnp.concatenate(
            [own_ref[:, real], own_ref[:, imag], far_ref[:, real], far_ref[:, imag]], axis=0
        )
        part = product(rows_split(rows), cols_split(piece[...]))
        total = part if total is None else total + part
    own_out[...] = total[:BND] + twist(total[BND : 2 * BND])
    far_out[...] = total[2 * BND : 3 * BND] + twist(total[3 * BND :])


def spread_kernel(own_tree, far_tree, *refs):
    pieces, (own_mat, far_mat, own_out, far_out, sol) = refs[:-5], refs[-5:]
    x, z, c = lax.axis_index(X), lax.axis_index(Z), lax.axis_index(C)
    for i, piece in enumerate(pieces):
        sol[i] = piece[...]
    for tree, mat, out in ((own_tree, own_mat, own_out), (far_tree, far_mat, far_out)):
        both = []
        for p in range(P_SIZE):
            block = tree[p]
            side = lax.rem((block // 2) % 2 + z, 2)
            slot = owner_slot(jnp.bitwise_xor(block // 4, x), c) * 2 + side
            field = sol[slot] * (block % 2 == c).astype(F32)
            both += [field, twist(field)]
        out[...] = product(rows_split(mat[...]), cols_split(jnp.concatenate(both, axis=0)))


def out_kernel(patt_ref, near_ref, far_ref, y_ref, g_ref, z_ref, out_ref):
    z = near_ref[...] + far_ref[...]
    z_ref[...] = z
    tail = cols_split(tail_field(z))
    for i in range(2):
        at = slice(i * BLK, (i + 1) * BLK)
        cols = tail_columns(g_ref[at, :], patt_ref, BROWS - 2 + i)
        out_ref[at, :] = y_ref[0, at, :] - product(rows_split(cols), tail)


STEPS = 2
STEP_ROWS = LEAF // STEPS
GROUP = 2


def bulk_kernel(step, patt_ref, src_ref, g_ref, first_ref, second_ref, cols_ref):
    def take(block):
        at = pl.ds(pl.multiple_of(block * BLK, BLK), BLK)
        return src_ref[0, 0, at, :], src_ref[1, 0, at, :]

    def some(n, carry):
        for i in range(GROUP):
            local = n * GROUP + i
            at = pl.ds(pl.multiple_of(local * BLK, BLK), BLK)
            low = pl.ds(pl.multiple_of(STEP_ROWS + local * BLK, BLK), BLK)
            row = step * (STEP_ROWS // BLK) + local
            g = g_ref[at, :]
            y = front_rows(g, gathered(patt_ref, row, take))
            first_ref[at, :] = y[:, :BND]
            second_ref[at, :] = y[:, BND:]
            cols_ref[at, :], cols_ref[low, :] = split(tail_columns(g, patt_ref, row))
        return carry

    lax.fori_loop(0, STEP_ROWS // BLK // GROUP, some, 0)


def field_kernel(near_ref, far_ref, *refs):
    y_refs, col_refs, out_ref = refs[:STEPS], refs[STEPS : 2 * STEPS], refs[-1]
    tail = cols_split(tail_field(near_ref[...] + far_ref[...]))
    for i in range(STEPS):
        at = slice(i * STEP_ROWS, (i + 1) * STEP_ROWS)
        out_ref[0, at, :] = y_refs[i][...] - product(col_refs[i][...], tail)


VM = pl.BlockSpec(memory_space=pltpu.VMEM)
SM = pl.BlockSpec(memory_space=pltpu.SMEM)


def shape(*dims):
    return jax.ShapeDtypeStruct(dims, F32)


ROOM = pltpu.CompilerParams(vmem_limit_bytes=12 << 20)


def cost(flops, size):
    return pl.CostEstimate(flops=flops, bytes_accessed=size, transcendentals=0)


def shifted(value, axis, distance):
    size = lax.axis_size(axis)
    return lax.ppermute(value, axis, [(i, (i + distance) % size) for i in range(size)])


def swapped(value, axis):
    return shifted(value, axis, 1)


HB = pl.BlockSpec(memory_space=pl.ANY)
FULL = pltpu.CompilerParams(vmem_limit_bytes=66_000_000)
NEAR1 = (1, 0, 3, 2)
NEAR3 = (3, 2, 1, 0)


def beside(value, turn):
    route = []
    for x in range(NX):
        for c in range(2):
            route.append((2 * x + c, 2 * (NEAR1, NEAR3)[(turn + c) % 2][x] + c))
    return lax.ppermute(value, (X, C), route)


def sweep(sources, front_inv, pattern, tree, lift, spread, couple, sep_inv, inflow):
    gmat, own_tree, patt = front_inv[0], tree[0, 0], pattern[0].T
    own_lift, own_spread, kmat, own_sep = lift[0], spread[0], couple[0], sep_inv[0]
    whole = lambda *dims: pl.BlockSpec(dims, lambda *i: (0,) * len(dims))
    block, double = shape(BND, BND), shape(2 * BND, BND)

    far_tree = swapped(own_tree, C)
    far_lift = swapped(own_lift, C)
    far_sep = swapped(own_sep, C)
    far_spread = swapped(own_spread, C)

    ytail, drive, gtail = pl.pallas_call(
        start_kernel,
        in_specs=[SM, HB, HB, HB, HB],
        out_specs=[VM, VM, VM],
        out_shape=[shape(2, BND, BND), block, shape(BND, NB * 2 * BLK)],
        scratch_shapes=[
            pltpu.VMEM((2 * NB, 2, BLK, BND), F32),
            pltpu.VMEM((BND, NB * 2 * BLK), F32),
            pltpu.VMEM((BND, 2 * BND), F32),
            pltpu.VMEM((BND, BND), F32),
            pltpu.SemaphoreType.DMA((3 + 2 * NB,)),
        ],
        compiler_params=FULL,
        cost_estimate=cost(2 * 128 * 512 * 256 * 6, 1 << 21),
        name="start",
    )(patt, sources, front_inv, couple, inflow)

    ys, cols = [], []
    for step in range(STEPS):
        y0, y1, col = pl.pallas_call(
            functools.partial(bulk_kernel, step),
            grid=(1,),
            in_specs=[
                SM,
                whole(2, 1, LEAF, BND),
                pl.BlockSpec((STEP_ROWS, NB * 2 * BLK), lambda i, step=step: (step, 0)),
            ],
            out_specs=[
                whole(STEP_ROWS, BND),
                whole(STEP_ROWS, BND),
                whole(2 * STEP_ROWS, 2 * BND),
            ],
            out_shape=[
                shape(STEP_ROWS, BND),
                shape(STEP_ROWS, BND),
                jax.ShapeDtypeStruct((2 * STEP_ROWS, 2 * BND), BF16),
            ],
            compiler_params=ROOM,
            cost_estimate=cost(2 * 512 * 512 * 256 * 6, 3 << 20),
        )(patt, sources, gmat)
        ys.append((y0, y1))
        cols.append(col)

    def tail_of(beat):
        return pl.BlockSpec((1, BND, BND), lambda i, beat=beat: (beat, 0, 0))

    result = None
    for beat in range(BEATS):
        if beat:
            devices = lax.axis_size("slab")
            incoming = lax.ppermute(outgoing, "slab", [(i, i + 1) for i in range(devices - 1)])
            drive = pl.pallas_call(
                drive_kernel,
                grid=(1,),
                in_specs=[whole(BND, 2 * BND), whole(BND, BND), tail_of(beat)],
                out_specs=whole(BND, BND),
                out_shape=block,
                compiler_params=ROOM,
                cost_estimate=cost(2 * 128 * 256 * 128 * 4, 1 << 18),
            )(kmat, incoming, ytail)
        far_drive = swapped(drive, C)
        pieces = pl.pallas_call(
            lift_kernel,
            in_specs=[SM, SM, VM, VM, VM, VM],
            out_specs=[VM] * NX,
            out_shape=[double] * NX,
            scratch_shapes=[pltpu.VMEM((2 * NX, BND, BND), F32)],
            compiler_params=ROOM,
            cost_estimate=cost(2 * 512 * 256 * 128 * 4, 3 << 19),
        )(own_tree, far_tree, drive, far_drive, own_lift, far_lift)
        came3 = beside(pieces[3], 1)
        came2 = beside(pieces[2], 1)
        came1 = beside(pieces[1] + came3, 0)
        near = (pieces[0] + came2) + came1
        mine = near + swapped(near, Z)
        first = beside(mine, 0)
        second = beside(mine, 1)
        third = beside(first, 1)
        own_part, far_part = pl.pallas_call(
            sep_kernel,
            in_specs=[VM] * (NX + 2),
            out_specs=[VM] * 2,
            out_shape=[block] * 2,
            compiler_params=ROOM,
            cost_estimate=cost(2 * 256 * 2048 * 128 * 4, 5 << 20),
        )(mine, first, second, third, own_sep, far_sep)
        sol = own_part + swapped(far_part, C)
        other = swapped(sol, Z)
        held = [None] * (2 * NX)
        for j, part in enumerate((sol, other)):
            held[j] = part
            held[2 + j] = beside(part, 0)
            held[4 + j] = beside(part, 1)
            held[6 + j] = beside(held[2 + j], 1)
        own_z, far_z = pl.pallas_call(
            spread_kernel,
            in_specs=[SM, SM] + [VM] * (2 * NX + 2),
            out_specs=[VM] * 2,
            out_shape=[block] * 2,
            scratch_shapes=[pltpu.VMEM((2 * NX, BND, BND), F32)],
            compiler_params=ROOM,
            cost_estimate=cost(2 * 128 * 1024 * 128 * 4, 3 << 19),
        )(own_tree, far_tree, *held, own_spread, far_spread)
        came = swapped(far_z, C)
        if beat == 0:
            _, outgoing = pl.pallas_call(
                out_kernel,
                grid=(1,),
                in_specs=[
                    SM,
                    whole(BND, BND),
                    whole(BND, BND),
                    tail_of(0),
                    whole(BND, NB * 2 * BLK),
                ],
                out_specs=[whole(BND, BND)] * 2,
                out_shape=[block] * 2,
                compiler_params=ROOM,
                cost_estimate=cost(2 * 128 * 256 * 128 * 4, 1 << 19),
                name="outgoing",
            )(patt, own_z, came, ytail, gtail)
        earlier = () if result is None else (result,)
        result = pl.pallas_call(
            field_kernel,
            grid=(1,),
            in_specs=[whole(BND, BND), whole(BND, BND)]
            + [whole(STEP_ROWS, BND)] * STEPS
            + [whole(2 * STEP_ROWS, 2 * BND)] * STEPS
            + [pl.BlockSpec(memory_space=pl.ANY)] * len(earlier),
            out_specs=pl.BlockSpec((1, LEAF, BND), lambda i, beat=beat: (beat, 0, 0)),
            out_shape=shape(2, LEAF, BND),
            input_output_aliases={2 + 2 * STEPS: 0} if earlier else {},
            compiler_params=ROOM,
            cost_estimate=cost(2 * 1024 * 256 * 128 * 4, 3 << 20),
        )(own_z, came, *[y[beat] for y in ys], *cols, *earlier)
    return result[:, None]


def solution(mesh):
    torus = Mesh(
        mesh.devices.reshape(mesh.shape["slab"], 4, 2, 2), ("slab", "front_0", "front_1", "front_2")
    )
    in_specs = (
        P(None, "slab", FRONT, None),
        P("slab", FRONT, None),
        P("slab", FRONT, None),
        P("slab", FRONT, None),
        P("slab", FRONT, None),
        P("slab", FRONT, None),
        P("slab", FRONT, None),
        P("slab", FRONT, None),
        P("slab", FRONT, None),
    )
    out_specs = P(None, "slab", FRONT, None)
    return jax.shard_map(
        sweep, mesh=torus, in_specs=in_specs, out_specs=out_specs, check_vma=False
    )
```

```python
import functools

import jax
import jax.numpy as jnp
from jax import lax
from jax.experimental import pallas as pl
from jax.experimental.pallas import tpu as pltpu
from jax.sharding import Mesh
from jax.sharding import PartitionSpec as P

BEATS = 2
LEAF = 1024
SEP = 2048
BLK = 64
NB = 4
BND = 128
P_SIZE = 4
BROWS = LEAF // BLK
FRONT = ("front_0", "front_1", "front_2")
X, Z, C = FRONT
NX = 4
HALF = SEP // 2
QUARTER = HALF // NX
F32 = jnp.float32
BF16 = jnp.bfloat16


def twist(field):
    half = field.shape[-1] // 2
    lane = lax.broadcasted_iota(jnp.int32, field.shape, len(field.shape) - 1)
    turned = pltpu.roll(field, half, len(field.shape) - 1)
    return jnp.where(lane < half, -turned, turned)


def split(a):
    high = a.astype(BF16)
    low = (a - high.astype(F32)).astype(BF16)
    return high, low


def mm(a, b):
    return jnp.dot(a, b, preferred_element_type=F32)


def rows_split(a):
    return jnp.concatenate(split(a), axis=0)


def cols_split(b):
    return jnp.concatenate(split(b), axis=1)


def product(stacked, paired):
    rows, cols = stacked.shape[0] // 2, paired.shape[1] // 2
    full = mm(stacked, paired)
    return full[:rows, :cols] + (full[:rows, cols:] + full[rows:, :cols])


def packed(matrix, field):
    both = jnp.concatenate([field, twist(field)], axis=0)
    return product(rows_split(matrix), cols_split(both))


QUAD = 32


def is_first(field):
    lane = lax.broadcasted_iota(jnp.int32, field.shape, 1)
    return (lane // QUAD) % 2 == 0


def to_second(field):
    return pltpu.roll(field, QUAD, 1)


def to_first(field):
    return pltpu.roll(field, field.shape[1] - QUAD, 1)


def pair_of(first, second):
    return jnp.where(is_first(first), first, to_second(second))


def half_of(field, c):
    return jnp.where(c == 0, field, to_first(field))


def wide(field):
    high = field.astype(BF16).astype(F32)
    return pair_of(high, field - high).astype(BF16)


def narrow(full):
    rows = full.shape[0] // 2
    total = full[:rows] + full[rows:]
    return total + jnp.where(is_first(total), to_first(total), to_second(total))


def applied(matrix, field):
    both = jnp.concatenate([field, twist(field)], axis=0)
    return narrow(mm(rows_split(matrix), wide(both)))


def front_rows(g, field):
    gh, gl = split(g)
    fh, fl = split(field)
    rows = g.shape[0]
    first = mm(jnp.concatenate([gh, gl], axis=0), fh)
    return first[:rows] + (first[rows:] + mm(gh, fl))


def gathered(patt_ref, row, take):
    both = []
    for k in range(NB):
        a, b = take(patt_ref[k, row])
        both.append(jnp.concatenate([a, b], axis=1))
        both.append(jnp.concatenate([twist(a), twist(b)], axis=1))
    return jnp.concatenate(both, axis=0)


def tail_columns(g, patt_ref, row):
    parts = []
    for block in (BROWS - 2, BROWS - 1):
        total = jnp.zeros((BLK, 2 * BLK), F32)
        for k in range(NB):
            held = (patt_ref[k, row] == block).astype(F32)
            total = total + held * g[:, k * 2 * BLK : (k + 1) * 2 * BLK]
        parts.append(total)
    return jnp.concatenate(parts, axis=1)


def tail_field(z):
    tz = twist(z)
    return jnp.concatenate([z[:BLK], tz[:BLK], z[BLK:], tz[BLK:]], axis=0)


def start_kernel(
    patt_ref, src_ref, g_ref, couple_ref, wave_ref, keep_ref, send_ref, cols_ref, blocks, held, couple, wave, sems
):
    copies = [
        pltpu.make_async_copy(g_ref.at[0, pl.ds(LEAF - BND, BND), :], held, sems.at[0]),
        pltpu.make_async_copy(couple_ref.at[0], couple, sems.at[1]),
        pltpu.make_async_copy(wave_ref.at[0], wave, sems.at[2]),
    ]
    for i in range(2):
        for k in range(NB):
            at = pl.ds(pl.multiple_of(patt_ref[k, BROWS - 2 + i] * BLK, BLK), BLK)
            n = i * NB + k
            copies.append(
                pltpu.make_async_copy(src_ref.at[:, 0, at, :], blocks.at[n], sems.at[3 + n])
            )
    for copy in copies:
        copy.start()
    for copy in copies[1:3]:
        copy.wait()
    drive = packed(couple[...], wave[...])
    for copy in copies[:1] + copies[3:]:
        copy.wait()
    ys = []
    for i in range(2):
        at = slice(i * BLK, (i + 1) * BLK)
        both = []
        for k in range(NB):
            pair = blocks[i * NB + k]
            both.append(jnp.concatenate([pair[0], pair[1]], axis=1))
            both.append(jnp.concatenate([twist(pair[0]), twist(pair[1])], axis=1))
        ys.append(front_rows(held[at, :], jnp.concatenate(both, axis=0)))
        cols_ref[at, :] = tail_columns(held[at, :], patt_ref, BROWS - 2 + i)
    y = jnp.concatenate(ys, axis=0)
    y0, y1 = y[:, :BND], y[:, BND:]
    drive = drive - y0
    c = lax.axis_index(C)
    for out, which in ((keep_ref, c), (send_ref, 1 - c)):
        out[:BND] = pair_of(half_of(drive, which), half_of(y0, which))
        later = half_of(y1, which)
        out[BND:] = pair_of(later, later)


def owner_slot(distance, c):
    return jnp.where(distance == 1, 1 + c, jnp.where(distance == 3, 2 - c, (distance // 2) * 3))


def slot_distance(slot, c):
    return (0, 1 + 2 * c, 3 - 2 * c, 2)[slot]


def lift_kernel(beat, own_tree, far_tree, keep_ref, came_ref, own_lift, far_lift, *refs):
    acc = refs[-1]
    outs = refs[-4:-1]
    x, c = lax.axis_index(X), lax.axis_index(C)
    acc[...] = jnp.zeros_like(acc)
    if beat == 0:
        drives = keep_ref[:BND], came_ref[:BND]
    else:
        own_couple, far_couple, wave_ref = refs[:3]
        wave = wave_ref[...]
        drives = (
            applied(own_couple[...], wave) - keep_ref[BND:],
            applied(far_couple[...], to_first(wave)) - came_ref[BND:],
        )
    parts = [applied(mat[...], drive) for mat, drive in zip((own_lift, far_lift), drives)]
    first = is_first(parts[0][:BND]).astype(jnp.int32)
    for tree, part in zip((own_tree, far_tree), parts):
        for p in range(P_SIZE):
            block = tree[p]
            owner = (block % 8) // 2
            slot = owner_slot(jnp.bitwise_xor(owner, x), c) * 2 + block % 2
            term = part[p * BND : (p + 1) * BND]
            acc[slot] += jnp.where(first == 1 - block // 8, term, 0.0)

    at = 0
    for out in outs:
        for i in range(out.shape[0] // BND):
            out[i * BND : (i + 1) * BND] = acc[at]
            at += 1


def sep_kernel(*refs):
    pieces, (own_ref, far_ref, out_ref) = refs[:-3], refs[-3:]
    x, c = lax.axis_index(X), lax.axis_index(C)
    total = None
    for slot in range(NX):
        owner = jnp.bitwise_xor(x, slot_distance(slot, c))
        piece = pieces[slot // 2][slot % 2 * 2 * BND : (slot % 2 + 1) * 2 * BND]

        def columns(ref, base):
            return jnp.concatenate(
                [
                    ref[:, pl.ds(pl.multiple_of(base + at + owner * QUARTER, QUARTER), QUARTER)]
                    for at in (0, HALF)
                ],
                axis=1,
            )

        rows = jnp.concatenate(
            [columns(ref, base) for ref in (own_ref, far_ref) for base in (0, SEP)], axis=0
        )
        field = jnp.concatenate([piece, to_first(piece)], axis=0)
        part = mm(rows_split(rows), wide(field))
        total = part if total is None else total + part
    total = narrow(total)
    own = total[:BND] + twist(total[BND : 2 * BND])
    far = total[2 * BND : 3 * BND] + twist(total[3 * BND :])
    out_ref[...] = jnp.where(is_first(own), own, far)


def spread_kernel(beat, own_tree, far_tree, own_mat, far_mat, *refs):
    pieces, sol = refs[:NX], refs[-1]
    x, z, c = lax.axis_index(X), lax.axis_index(Z), lax.axis_index(C)
    for i, piece in enumerate(pieces):
        for k in range(2):
            sol[2 * (2 * (i // 2) + k) + i % 2] = piece[k * BND : (k + 1) * BND]
    zs = []
    for tree, mat in ((own_tree, own_mat), (far_tree, far_mat)):
        both = []
        for p in range(P_SIZE):
            block = tree[p]
            side = lax.rem((block // 2) % 2 + z, 2)
            slot = owner_slot(jnp.bitwise_xor(block // 4, x), c) * 2 + side
            field = sol[slot]
            field = jnp.where(block % 2 == c, field, to_first(field))
            both += [field, twist(field)]
        zs.append(narrow(mm(rows_split(mat[...]), wide(jnp.concatenate(both, axis=0)))))
    first = is_first(zs[0])
    if beat:
        refs[-2][:BND] = refs[NX][...]
        refs[-2][BND:] = jnp.where(first, zs[0], zs[1])
        return
    keep_ref, came_ref, own_cols, far_cols, z_ref, out_ref = refs[NX:-1]
    z_ref[...] = jnp.where(first, zs[0], zs[1])
    outs = []
    for held, cols, value in zip((keep_ref, came_ref), (own_cols, far_cols), zs):
        moved = narrow(mm(rows_split(cols[...]), wide(tail_field(value))))
        outs.append(held[:BND] - moved)
    out_ref[...] = jnp.where(first, to_first(outs[0]), outs[1])


STEPS = 2
STEP_ROWS = LEAF // STEPS
GROUP = 2


def bulk_kernel(step, patt_ref, src_ref, g_ref, first_ref, second_ref, cols_ref):
    def take(block):
        at = pl.ds(pl.multiple_of(block * BLK, BLK), BLK)
        return src_ref[0, 0, at, :], src_ref[1, 0, at, :]

    def some(n, carry):
        for i in range(GROUP):
            local = n * GROUP + i
            at = pl.ds(pl.multiple_of(local * BLK, BLK), BLK)
            low = pl.ds(pl.multiple_of(STEP_ROWS + local * BLK, BLK), BLK)
            row = step * (STEP_ROWS // BLK) + local
            g = g_ref[at, :]
            y = front_rows(g, gathered(patt_ref, row, take))
            first_ref[at, :] = y[:, :BND]
            second_ref[at, :] = y[:, BND:]
            cols_ref[at, :], cols_ref[low, :] = split(tail_columns(g, patt_ref, row))
        return carry

    lax.fori_loop(0, STEP_ROWS // BLK // GROUP, some, 0)


def field_kernel(own_ref, came_ref, *refs):
    y_refs, col_refs = refs[: 2 * STEPS], refs[2 * STEPS : 3 * STEPS]
    out_ref, buffer, sems = refs[3 * STEPS :]
    copies = []
    for beat in range(BEATS):
        own = own_ref[beat * BND : (beat + 1) * BND]
        came = came_ref[beat * BND : (beat + 1) * BND]
        first = is_first(own)
        z = jnp.where(
            lax.axis_index(C) == 0,
            jnp.where(first, own, came),
            jnp.where(first, to_first(came), to_second(own)),
        )
        tail = cols_split(tail_field(z))
        for i in range(STEPS):
            buffer[beat, i] = y_refs[2 * i + beat][...] - product(col_refs[i][...], tail)
            copy = pltpu.make_async_copy(
                buffer.at[beat, i],
                out_ref.at[beat, pl.ds(i * STEP_ROWS, STEP_ROWS), :],
                sems.at[beat, i],
            )
            copy.start()
            copies.append(copy)
    for copy in copies:
        copy.wait()


VM = pl.BlockSpec(memory_space=pltpu.VMEM)
SM = pl.BlockSpec(memory_space=pltpu.SMEM)


def shape(*dims):
    return jax.ShapeDtypeStruct(dims, F32)


ROOM = pltpu.CompilerParams(vmem_limit_bytes=12 << 20)


def cost(flops, size):
    return pl.CostEstimate(flops=flops, bytes_accessed=size, transcendentals=0)


def shifted(value, axis, distance):
    size = lax.axis_size(axis)
    return lax.ppermute(value, axis, [(i, (i + distance) % size) for i in range(size)])


def swapped(value, axis):
    return shifted(value, axis, 1)


HB = pl.BlockSpec(memory_space=pl.ANY)
FULL = pltpu.CompilerParams(vmem_limit_bytes=66_000_000)
NEAR1 = (1, 0, 3, 2)
NEAR3 = (3, 2, 1, 0)


def beside(value, turn):
    route = []
    for x in range(NX):
        for c in range(2):
            route.append((2 * x + c, 2 * (NEAR1, NEAR3)[(turn + c) % 2][x] + c))
    return lax.ppermute(value, (X, C), route)


def sweep(sources, front_inv, pattern, tree, lift, spread, couple, sep_inv, inflow):
    gmat, own_tree, patt = front_inv[0], tree[0, 0], pattern[0].T
    own_lift, own_spread, kmat, own_sep = lift[0], spread[0], couple[0], sep_inv[0]
    whole = lambda *dims: pl.BlockSpec(dims, lambda *i: (0,) * len(dims))
    block, double = shape(BND, BND), shape(2 * BND, BND)

    far_tree = swapped(own_tree, C)
    far_lift = swapped(own_lift, C)
    far_sep = swapped(own_sep, C)
    far_spread = swapped(own_spread, C)
    far_couple = swapped(kmat, C)

    keep, send, own_cols = pl.pallas_call(
        start_kernel,
        in_specs=[SM, HB, HB, HB, HB],
        out_specs=[VM, VM, VM],
        out_shape=[double, double, shape(BND, 2 * BND)],
        scratch_shapes=[
            pltpu.VMEM((2 * NB, 2, BLK, BND), F32),
            pltpu.VMEM((BND, NB * 2 * BLK), F32),
            pltpu.VMEM((BND, 2 * BND), F32),
            pltpu.VMEM((BND, BND), F32),
            pltpu.SemaphoreType.DMA((3 + 2 * NB,)),
        ],
        compiler_params=FULL,
        cost_estimate=cost(2 * 128 * 512 * 256 * 6, 1 << 21),
        name="start",
    )(patt, sources, front_inv, couple, inflow)
    came = swapped(send, C)
    far_cols = swapped(own_cols, C)

    ys, cols = [], []
    for step in range(STEPS):
        y0, y1, col = pl.pallas_call(
            functools.partial(bulk_kernel, step),
            grid=(1,),
            in_specs=[
                SM,
                whole(2, 1, LEAF, BND),
                pl.BlockSpec((STEP_ROWS, NB * 2 * BLK), lambda i, step=step: (step, 0)),
            ],
            out_specs=[
                whole(STEP_ROWS, BND),
                whole(STEP_ROWS, BND),
                whole(2 * STEP_ROWS, 2 * BND),
            ],
            out_shape=[
                shape(STEP_ROWS, BND),
                shape(STEP_ROWS, BND),
                jax.ShapeDtypeStruct((2 * STEP_ROWS, 2 * BND), BF16),
            ],
            compiler_params=ROOM,
            cost_estimate=cost(2 * 512 * 512 * 256 * 6, 3 << 20),
        )(patt, sources, gmat)
        ys.append((y0, y1))
        cols.append(col)

    for beat in range(BEATS):
        extra = ()
        if beat:
            devices = lax.axis_size("slab")
            incoming = lax.ppermute(outgoing, "slab", [(i, i + 1) for i in range(devices - 1)])
            extra = (kmat, far_couple, incoming)
        pieces = pl.pallas_call(
            functools.partial(lift_kernel, beat),
            in_specs=[SM, SM] + [VM] * (4 + len(extra)),
            out_specs=[VM] * 3,
            out_shape=[double, double, shape(4 * BND, BND)],
            scratch_shapes=[pltpu.VMEM((2 * NX, BND, BND), F32)],
            compiler_params=ROOM,
            cost_estimate=cost(2 * 512 * 256 * 128 * 4, 3 << 19),
        )(own_tree, far_tree, keep, came, own_lift, far_lift, *extra)
        outer = beside(pieces[2], 1)
        inner = beside(pieces[1] + outer[2 * BND :], 0)
        near = (pieces[0] + outer[: 2 * BND]) + inner
        mine = near + swapped(near, Z)
        inner = jnp.concatenate([mine, beside(mine, 0)], axis=0)
        outer = beside(inner, 1)
        sol = pl.pallas_call(
            sep_kernel,
            in_specs=[VM] * 4,
            out_specs=VM,
            out_shape=block,
            compiler_params=ROOM,
            cost_estimate=cost(2 * 256 * 2048 * 128 * 4, 5 << 20),
        )(inner, outer, own_sep, far_sep)
        other = swapped(sol, Z)
        held = [None] * NX
        for j, part in enumerate((sol, other)):
            held[j] = jnp.concatenate([part, beside(part, 0)], axis=0)
            held[2 + j] = beside(held[j], 1)
        extra = (zvals,) if beat else (keep, came, own_cols, far_cols)
        answer = pl.pallas_call(
            functools.partial(spread_kernel, beat),
            in_specs=[SM, SM] + [VM] * (NX + 2 + len(extra)),
            out_specs=[VM] * (2 - beat),
            out_shape=[double] if beat else [block] * 2,
            scratch_shapes=[pltpu.VMEM((2 * NX, BND, BND), F32)],
            compiler_params=ROOM,
            cost_estimate=cost(2 * 128 * 1024 * 128 * 4, 3 << 19),
        )(own_tree, far_tree, own_spread, far_spread, *held, *extra)
        zvals, outgoing = answer[0], answer[-1]
    zcame = swapped(zvals, C)
    result = pl.pallas_call(
        field_kernel,
        in_specs=[VM] * (2 + 3 * STEPS),
        out_specs=pl.BlockSpec(memory_space=pl.ANY),
        out_shape=shape(BEATS, LEAF, BND),
        scratch_shapes=[
            pltpu.VMEM((BEATS, STEPS, STEP_ROWS, BND), F32),
            pltpu.SemaphoreType.DMA((BEATS, STEPS)),
        ],
        compiler_params=ROOM,
        cost_estimate=cost(2 * 1024 * 256 * 256 * 4, 3 << 20),
        name="field",
    )(zvals, zcame, *ys[0], *ys[1], *cols)
    return result[:, None]


def solution(mesh):
    torus = Mesh(
        mesh.devices.reshape(mesh.shape["slab"], 4, 2, 2), ("slab", "front_0", "front_1", "front_2")
    )
    in_specs = (
        P(None, "slab", FRONT, None),
        P("slab", FRONT, None),
        P("slab", FRONT, None),
        P("slab", FRONT, None),
        P("slab", FRONT, None),
        P("slab", FRONT, None),
        P("slab", FRONT, None),
        P("slab", FRONT, None),
        P("slab", FRONT, None),
    )
    out_specs = P(None, "slab", FRONT, None)
    return jax.shard_map(sweep, mesh=torus, in_specs=in_specs, out_specs=out_specs, check_vma=False)
```

```python
import functools

import jax
import jax.numpy as jnp
from jax import lax
from jax.experimental import pallas as pl
from jax.experimental.pallas import tpu as pltpu
from jax.sharding import Mesh
from jax.sharding import PartitionSpec as P

BEATS = 2
LEAF = 1024
SEP = 2048
BLK = 64
NB = 4
BND = 128
P_SIZE = 4
BROWS = LEAF // BLK
FRONT = ("front_0", "front_1", "front_2")
X, Z, C = FRONT
NX = 4
HALF = SEP // 2
QUARTER = HALF // NX
F32 = jnp.float32
BF16 = jnp.bfloat16


def twist(field):
    half = field.shape[-1] // 2
    lane = lax.broadcasted_iota(jnp.int32, field.shape, len(field.shape) - 1)
    turned = pltpu.roll(field, half, len(field.shape) - 1)
    return jnp.where(lane < half, -turned, turned)


def split(a):
    high = a.astype(BF16)
    low = (a - high.astype(F32)).astype(BF16)
    return high, low


def mm(a, b):
    return jnp.dot(a, b, preferred_element_type=F32)


def rows_split(a):
    return jnp.concatenate(split(a), axis=0)


def cols_split(b):
    return jnp.concatenate(split(b), axis=1)


def product(stacked, paired):
    rows, cols = stacked.shape[0] // 2, paired.shape[1] // 2
    full = mm(stacked, paired)
    return full[:rows, :cols] + (full[:rows, cols:] + full[rows:, :cols])


def packed(matrix, field):
    both = jnp.concatenate([field, twist(field)], axis=0)
    return product(rows_split(matrix), cols_split(both))


QUAD = 32


def is_first(field):
    lane = lax.broadcasted_iota(jnp.int32, field.shape, 1)
    return (lane // QUAD) % 2 == 0


def to_second(field):
    return pltpu.roll(field, QUAD, 1)


def to_first(field):
    return pltpu.roll(field, field.shape[1] - QUAD, 1)


def pair_of(first, second):
    return jnp.where(is_first(first), first, to_second(second))


def half_of(field, c):
    return jnp.where(c == 0, field, to_first(field))


def wide(field):
    high = field.astype(BF16).astype(F32)
    return pair_of(high, field - high).astype(BF16)


def narrow(full):
    rows = full.shape[0] // 2
    total = full[:rows] + full[rows:]
    return total + jnp.where(is_first(total), to_first(total), to_second(total))


def applied(matrix, field):
    both = jnp.concatenate([field, twist(field)], axis=0)
    return narrow(mm(rows_split(matrix), wide(both)))


def front_rows(g, field):
    gh, gl = split(g)
    fh, fl = split(field)
    rows = g.shape[0]
    first = mm(jnp.concatenate([gh, gl], axis=0), fh)
    return first[:rows] + (first[rows:] + mm(gh, fl))


def gathered(patt_ref, row, take):
    both = []
    for k in range(NB):
        a, b = take(patt_ref[k, row])
        both.append(jnp.concatenate([a, b], axis=1))
        both.append(jnp.concatenate([twist(a), twist(b)], axis=1))
    return jnp.concatenate(both, axis=0)


def tail_columns(g, patt_ref, row):
    parts = []
    for block in (BROWS - 2, BROWS - 1):
        total = jnp.zeros((BLK, 2 * BLK), F32)
        for k in range(NB):
            held = (patt_ref[k, row] == block).astype(F32)
            total = total + held * g[:, k * 2 * BLK : (k + 1) * 2 * BLK]
        parts.append(total)
    return jnp.concatenate(parts, axis=1)


def tail_field(z):
    tz = twist(z)
    return jnp.concatenate([z[:BLK], tz[:BLK], z[BLK:], tz[BLK:]], axis=0)


def start_kernel(
    patt_ref, src_ref, g_ref, couple_ref, wave_ref, keep_ref, send_ref, cols_ref, blocks, held, couple, wave, sems
):
    copies = [
        pltpu.make_async_copy(g_ref.at[0, pl.ds(LEAF - BND, BND), :], held, sems.at[0]),
        pltpu.make_async_copy(couple_ref.at[0], couple, sems.at[1]),
        pltpu.make_async_copy(wave_ref.at[0], wave, sems.at[2]),
    ]
    for i in range(2):
        for k in range(NB):
            at = pl.ds(pl.multiple_of(patt_ref[k, BROWS - 2 + i] * BLK, BLK), BLK)
            n = i * NB + k
            copies.append(
                pltpu.make_async_copy(src_ref.at[:, 0, at, :], blocks.at[n], sems.at[3 + n])
            )
    for copy in copies:
        copy.start()
    for copy in copies[1:3]:
        copy.wait()
    drive = packed(couple[...], wave[...])
    for copy in copies[:1] + copies[3:]:
        copy.wait()
    ys = []
    for i in range(2):
        at = slice(i * BLK, (i + 1) * BLK)
        both = []
        for k in range(NB):
            pair = blocks[i * NB + k]
            both.append(jnp.concatenate([pair[0], pair[1]], axis=1))
            both.append(jnp.concatenate([twist(pair[0]), twist(pair[1])], axis=1))
        ys.append(front_rows(held[at, :], jnp.concatenate(both, axis=0)))
        cols_ref[at, :] = tail_columns(held[at, :], patt_ref, BROWS - 2 + i)
    y = jnp.concatenate(ys, axis=0)
    y0, y1 = y[:, :BND], y[:, BND:]
    drive = drive - y0
    c = lax.axis_index(C)
    for out, which in ((keep_ref, c), (send_ref, 1 - c)):
        out[:BND] = pair_of(half_of(drive, which), half_of(y0, which))
        later = half_of(y1, which)
        out[BND:] = pair_of(later, later)


def lift_kernel(beat, own_tree, far_tree, keep_ref, came_ref, own_lift, far_lift, *refs):
    copies = ()
    if beat == 0:
        *refs, lift_here, tree_here, sems = refs
        copies = (
            pltpu.make_async_copy(own_lift, lift_here, sems.at[0]),
            pltpu.make_async_copy(own_tree, tree_here, sems.at[1]),
        )
        for copy in copies:
            copy.start()
        own_lift, own_tree = lift_here, tree_here
    acc = refs[-1]
    outs = refs[-1 - NX : -1]
    x = lax.axis_index(X)
    acc[...] = jnp.zeros_like(acc)
    if beat == 0:
        drives = keep_ref[:BND], came_ref[:BND]
    else:
        own_couple, far_couple, wave_ref = refs[:3]
        wave = wave_ref[...]
        drives = (
            applied(own_couple[...], wave) - keep_ref[BND:],
            applied(far_couple[...], to_first(wave)) - came_ref[BND:],
        )
    far_part = applied(far_lift[...], drives[1])
    for copy in copies:
        copy.wait()
    parts = [applied(own_lift[...], drives[0]), far_part]
    first = is_first(parts[0][:BND]).astype(jnp.int32)
    for tree, part in zip((own_tree, far_tree), parts):
        for p in range(P_SIZE):
            block = tree[p]
            owner = (block % 8) // 2
            slot = lax.rem(owner - x + NX, NX) * 2 + block % 2
            term = part[p * BND : (p + 1) * BND]
            acc[slot] += jnp.where(first == 1 - block // 8, term, 0.0)

    at = 0
    for out in outs:
        for i in range(out.shape[0] // BND):
            out[i * BND : (i + 1) * BND] = acc[at]
            at += 1


def sep_kernel(*refs):
    pieces, (own_ref, far_ref, out_ref) = refs[:-3], refs[-3:]
    x = lax.axis_index(X)
    total = None
    for slot in range(NX):
        owner = lax.rem(x - slot + NX, NX)
        piece = pieces[slot][...]

        def columns(ref, base):
            return jnp.concatenate(
                [
                    ref[:, pl.ds(pl.multiple_of(base + at + owner * QUARTER, QUARTER), QUARTER)]
                    for at in (0, HALF)
                ],
                axis=1,
            )

        rows = jnp.concatenate(
            [columns(ref, base) for ref in (own_ref, far_ref) for base in (0, SEP)], axis=0
        )
        field = jnp.concatenate([piece, to_first(piece)], axis=0)
        part = mm(rows_split(rows), wide(field))
        total = part if total is None else total + part
    total = narrow(total)
    own = total[:BND] + twist(total[BND : 2 * BND])
    far = total[2 * BND : 3 * BND] + twist(total[3 * BND :])
    out_ref[...] = jnp.where(is_first(own), own, far)


def spread_kernel(beat, own_tree, far_tree, own_mat, far_mat, *refs):
    pieces, sol = refs[: 2 * NX], refs[-1]
    x, z, c = lax.axis_index(X), lax.axis_index(Z), lax.axis_index(C)
    for i, piece in enumerate(pieces):
        sol[i] = piece[...]
    zs = []
    for tree, mat in ((own_tree, own_mat), (far_tree, far_mat)):
        both = []
        for p in range(P_SIZE):
            block = tree[p]
            side = lax.rem((block // 2) % 2 + z, 2)
            slot = lax.rem(x - block // 4 + NX, NX)
            field = sol[side * NX + slot]
            field = jnp.where(block % 2 == c, field, to_first(field))
            both += [field, twist(field)]
        zs.append(narrow(mm(rows_split(mat[...]), wide(jnp.concatenate(both, axis=0)))))
    first = is_first(zs[0])
    if beat:
        refs[-2][:BND] = refs[2 * NX][...]
        refs[-2][BND:] = jnp.where(first, zs[0], zs[1])
        return
    keep_ref, came_ref, own_cols, far_cols, z_ref, out_ref = refs[2 * NX : -1]
    z_ref[...] = jnp.where(first, zs[0], zs[1])
    outs = []
    for held, cols, value in zip((keep_ref, came_ref), (own_cols, far_cols), zs):
        moved = narrow(mm(rows_split(cols[...]), wide(tail_field(value))))
        outs.append(held[:BND] - moved)
    out_ref[...] = jnp.where(first, to_first(outs[0]), outs[1])


STEPS = 2
STEP_ROWS = LEAF // STEPS
GROUP = 2


def bulk_kernel(step, patt_ref, src_ref, g_ref, first_ref, second_ref, cols_ref):
    def take(block):
        at = pl.ds(pl.multiple_of(block * BLK, BLK), BLK)
        return src_ref[0, 0, at, :], src_ref[1, 0, at, :]

    def some(n, carry):
        for i in range(GROUP):
            local = n * GROUP + i
            at = pl.ds(pl.multiple_of(local * BLK, BLK), BLK)
            low = pl.ds(pl.multiple_of(STEP_ROWS + local * BLK, BLK), BLK)
            row = step * (STEP_ROWS // BLK) + local
            g = g_ref[at, :]
            y = front_rows(g, gathered(patt_ref, row, take))
            first_ref[at, :] = y[:, :BND]
            second_ref[at, :] = y[:, BND:]
            cols_ref[at, :], cols_ref[low, :] = split(tail_columns(g, patt_ref, row))
        return carry

    lax.fori_loop(0, STEP_ROWS // BLK // GROUP, some, 0)


def field_kernel(own_ref, came_ref, *refs):
    y_refs, col_refs = refs[: 2 * STEPS], refs[2 * STEPS : 3 * STEPS]
    out_ref, buffer, sems = refs[3 * STEPS :]
    copies = []
    for beat in range(BEATS):
        own = own_ref[beat * BND : (beat + 1) * BND]
        came = came_ref[beat * BND : (beat + 1) * BND]
        first = is_first(own)
        z = jnp.where(
            lax.axis_index(C) == 0,
            jnp.where(first, own, came),
            jnp.where(first, to_first(came), to_second(own)),
        )
        tail = cols_split(tail_field(z))
        for i in range(STEPS):
            buffer[beat, i] = y_refs[2 * i + beat][...] - product(col_refs[i][...], tail)
            copy = pltpu.make_async_copy(
                buffer.at[beat, i],
                out_ref.at[beat, pl.ds(i * STEP_ROWS, STEP_ROWS), :],
                sems.at[beat, i],
            )
            copy.start()
            copies.append(copy)
    for copy in copies:
        copy.wait()


VM = pl.BlockSpec(memory_space=pltpu.VMEM)
SM = pl.BlockSpec(memory_space=pltpu.SMEM)


def shape(*dims):
    return jax.ShapeDtypeStruct(dims, F32)


ROOM = pltpu.CompilerParams(vmem_limit_bytes=12 << 20)


def cost(flops, size):
    return pl.CostEstimate(flops=flops, bytes_accessed=size, transcendentals=0)


def shifted(value, axis, distance):
    size = lax.axis_size(axis)
    return lax.ppermute(value, axis, [(i, (i + distance) % size) for i in range(size)])


def swapped(value, axis):
    return shifted(value, axis, 1)


HB = pl.BlockSpec(memory_space=pltpu.HBM)


def in_hbm(value):
    return pltpu.with_memory_space_constraint(value, pltpu.HBM)


def around(pieces):
    got = [pieces[0]] + [None] * (NX - 1)
    for d in (2, 1, 3):
        got[d] = shifted(pieces[d], X, d)
    return got


def sweep(sources, front_inv, pattern, tree, lift, spread, couple, sep_inv, inflow):
    gmat, own_tree, patt = front_inv[0], tree[0, 0], pattern[0].T
    own_lift, own_spread, kmat, own_sep = lift[0], spread[0], couple[0], sep_inv[0]
    whole = lambda *dims: pl.BlockSpec(dims, lambda *i: (0,) * len(dims))
    block, double = shape(BND, BND), shape(2 * BND, BND)

    far_tree = swapped(own_tree, C)
    far_lift = swapped(own_lift, C)
    far_sep = swapped(own_sep, C)
    far_spread = swapped(own_spread, C)
    far_couple = swapped(kmat, C)

    keep, send, own_cols = pl.pallas_call(
        start_kernel,
        in_specs=[SM, HB, HB, HB, HB],
        out_specs=[VM, VM, VM],
        out_shape=[double, double, shape(BND, 2 * BND)],
        scratch_shapes=[
            pltpu.VMEM((2 * NB, 2, BLK, BND), F32),
            pltpu.VMEM((BND, NB * 2 * BLK), F32),
            pltpu.VMEM((BND, 2 * BND), F32),
            pltpu.VMEM((BND, BND), F32),
            pltpu.SemaphoreType.DMA((3 + 2 * NB,)),
        ],
        compiler_params=ROOM,
        cost_estimate=cost(2 * 128 * 512 * 256 * 6, 1 << 21),
        name="start",
    )(patt, *[in_hbm(a) for a in (sources, front_inv, couple, inflow)])
    came = swapped(send, C)
    far_cols = swapped(own_cols, C)

    ys, cols = [], []
    for step in range(STEPS):
        y0, y1, col = pl.pallas_call(
            functools.partial(bulk_kernel, step),
            grid=(1,),
            in_specs=[
                SM,
                whole(2, 1, LEAF, BND),
                pl.BlockSpec((STEP_ROWS, NB * 2 * BLK), lambda i, step=step: (step, 0)),
            ],
            out_specs=[
                whole(STEP_ROWS, BND),
                whole(STEP_ROWS, BND),
                whole(2 * STEP_ROWS, 2 * BND),
            ],
            out_shape=[
                shape(STEP_ROWS, BND),
                shape(STEP_ROWS, BND),
                jax.ShapeDtypeStruct((2 * STEP_ROWS, 2 * BND), BF16),
            ],
            compiler_params=ROOM,
            cost_estimate=cost(2 * 512 * 512 * 256 * 6, 3 << 20),
        )(patt, sources, gmat)
        ys.append((y0, y1))
        cols.append(col)

    for beat in range(BEATS):
        extra = ()
        if beat:
            devices = lax.axis_size("slab")
            incoming = lax.ppermute(outgoing, "slab", [(i, i + 1) for i in range(devices - 1)])
            extra = (kmat, far_couple, incoming)
        fetched = [
            pltpu.VMEM((P_SIZE * BND, 2 * BND), F32),
            pltpu.SMEM((P_SIZE,), jnp.int32),
            pltpu.SemaphoreType.DMA((2,)),
        ]
        fetched = [] if beat else fetched
        pieces = pl.pallas_call(
            functools.partial(lift_kernel, beat),
            in_specs=[SM if beat else HB, SM, VM, VM, VM if beat else HB] + [VM] * (1 + len(extra)),
            out_specs=[VM] * NX,
            out_shape=[double] * NX,
            scratch_shapes=[pltpu.VMEM((2 * NX, BND, BND), F32)] + fetched,
            compiler_params=ROOM,
            cost_estimate=cost(2 * 512 * 256 * 128 * 4, 3 << 19),
        )(
            own_tree if beat else in_hbm(own_tree),
            far_tree,
            keep,
            came,
            own_lift if beat else in_hbm(own_lift),
            far_lift,
            *extra,
        )
        got = around(pieces)
        near = (pieces[0] + got[1]) + (got[2] + got[3])
        mine = near + swapped(near, Z)
        held = around([mine] * NX)
        sol = pl.pallas_call(
            sep_kernel,
            in_specs=[VM] * (NX + 2),
            out_specs=VM,
            out_shape=block,
            compiler_params=ROOM,
            cost_estimate=cost(2 * 256 * 2048 * 128 * 4, 5 << 20),
        )(*held, own_sep, far_sep)
        other = swapped(sol, Z)
        held = around([sol] * NX) + around([other] * NX)
        extra = (zvals,) if beat else (keep, came, own_cols, far_cols)
        answer = pl.pallas_call(
            functools.partial(spread_kernel, beat),
            in_specs=[SM, SM] + [VM] * (2 * NX + 2 + len(extra)),
            out_specs=[VM] * (2 - beat),
            out_shape=[double] if beat else [block] * 2,
            scratch_shapes=[pltpu.VMEM((2 * NX, BND, BND), F32)],
            compiler_params=ROOM,
            cost_estimate=cost(2 * 128 * 1024 * 128 * 4, 3 << 19),
        )(own_tree, far_tree, own_spread, far_spread, *held, *extra)
        zvals, outgoing = answer[0], answer[-1]
    zcame = swapped(zvals, C)
    result = pl.pallas_call(
        field_kernel,
        in_specs=[VM] * (2 + 3 * STEPS),
        out_specs=pl.BlockSpec(memory_space=pl.ANY),
        out_shape=shape(BEATS, LEAF, BND),
        scratch_shapes=[
            pltpu.VMEM((BEATS, STEPS, STEP_ROWS, BND), F32),
            pltpu.SemaphoreType.DMA((BEATS, STEPS)),
        ],
        compiler_params=ROOM,
        cost_estimate=cost(2 * 1024 * 256 * 256 * 4, 3 << 20),
        name="field",
    )(zvals, zcame, *ys[0], *ys[1], *cols)
    return result[:, None]


def solution(mesh):
    torus = Mesh(
        mesh.devices.reshape(mesh.shape["slab"], 4, 2, 2), ("slab", "front_0", "front_1", "front_2")
    )
    in_specs = (
        P(None, "slab", FRONT, None),
        P("slab", FRONT, None),
        P("slab", FRONT, None),
        P("slab", FRONT, None),
        P("slab", FRONT, None),
        P("slab", FRONT, None),
        P("slab", FRONT, None),
        P("slab", FRONT, None),
        P("slab", FRONT, None),
    )
    out_specs = P(None, "slab", FRONT, None)
    return jax.shard_map(sweep, mesh=torus, in_specs=in_specs, out_specs=out_specs, check_vma=False)
```

```python
import functools

import jax
import jax.numpy as jnp
from jax import lax
from jax.experimental import pallas as pl
from jax.experimental.pallas import tpu as pltpu
from jax.sharding import Mesh
from jax.sharding import PartitionSpec as P

BEATS = 2
LEAF = 1024
SEP = 2048
BLK = 64
NB = 4
BND = 128
P_SIZE = 4
BROWS = LEAF // BLK
FRONT = ("front_0", "front_1", "front_2")
X, Z, C = FRONT
NX = 4
HALF = SEP // 2
QUARTER = HALF // NX
F32 = jnp.float32
BF16 = jnp.bfloat16


def twist(field):
    half = field.shape[-1] // 2
    lane = lax.broadcasted_iota(jnp.int32, field.shape, len(field.shape) - 1)
    turned = pltpu.roll(field, half, len(field.shape) - 1)
    return jnp.where(lane < half, -turned, turned)


def split(a):
    high = a.astype(BF16)
    low = (a - high.astype(F32)).astype(BF16)
    return high, low


def mm(a, b):
    return jnp.dot(a, b, preferred_element_type=F32)


def rows_split(a):
    return jnp.concatenate(split(a), axis=0)


def cols_split(b):
    return jnp.concatenate(split(b), axis=1)


def product(stacked, paired):
    rows, cols = stacked.shape[0] // 2, paired.shape[1] // 2
    full = mm(stacked, paired)
    return full[:rows, :cols] + (full[:rows, cols:] + full[rows:, :cols])


def packed(matrix, field):
    both = jnp.concatenate([field, twist(field)], axis=0)
    return product(rows_split(matrix), cols_split(both))


QUAD = 32


def is_first(field):
    lane = lax.broadcasted_iota(jnp.int32, field.shape, 1)
    return (lane // QUAD) % 2 == 0


def to_second(field):
    return pltpu.roll(field, QUAD, 1)


def to_first(field):
    return pltpu.roll(field, field.shape[1] - QUAD, 1)


def pair_of(first, second):
    return jnp.where(is_first(first), first, to_second(second))


def half_of(field, c):
    return jnp.where(c == 0, field, to_first(field))


def wide(field):
    high = field.astype(BF16).astype(F32)
    return pair_of(high, field - high).astype(BF16)


def narrow(full):
    rows = full.shape[0] // 2
    total = full[:rows] + full[rows:]
    return total + jnp.where(is_first(total), to_first(total), to_second(total))


def applied(matrix, field):
    both = jnp.concatenate([field, twist(field)], axis=0)
    return narrow(mm(rows_split(matrix), wide(both)))


def front_rows(g, field):
    gh, gl = split(g)
    fh, fl = split(field)
    rows = g.shape[0]
    first = mm(jnp.concatenate([gh, gl], axis=0), fh)
    return first[:rows] + (first[rows:] + mm(gh, fl))


def gathered(patt_ref, row, take):
    both = []
    for k in range(NB):
        a, b = take(patt_ref[k, row])
        both.append(jnp.concatenate([a, b], axis=1))
        both.append(jnp.concatenate([twist(a), twist(b)], axis=1))
    return jnp.concatenate(both, axis=0)


def tail_columns(g, patt_ref, row):
    parts = []
    for block in (BROWS - 2, BROWS - 1):
        total = jnp.zeros((BLK, 2 * BLK), F32)
        for k in range(NB):
            held = (patt_ref[k, row] == block).astype(F32)
            total = total + held * g[:, k * 2 * BLK : (k + 1) * 2 * BLK]
        parts.append(total)
    return jnp.concatenate(parts, axis=1)


def tail_field(z):
    tz = twist(z)
    return jnp.concatenate([z[:BLK], tz[:BLK], z[BLK:], tz[BLK:]], axis=0)


def start_kernel(
    patt_ref, src_ref, g_ref, couple_ref, wave_ref, lift_ref, keep_ref, send_ref, cols_ref, lift_out, blocks, held, couple, wave, sems
):
    copies = [
        pltpu.make_async_copy(g_ref.at[0, pl.ds(LEAF - BND, BND), :], held, sems.at[0]),
        pltpu.make_async_copy(couple_ref.at[0], couple, sems.at[1]),
        pltpu.make_async_copy(wave_ref.at[0], wave, sems.at[2]),
    ]
    for i in range(2):
        for k in range(NB):
            at = pl.ds(pl.multiple_of(patt_ref[k, BROWS - 2 + i] * BLK, BLK), BLK)
            n = i * NB + k
            copies.append(
                pltpu.make_async_copy(src_ref.at[:, 0, at, :], blocks.at[n], sems.at[3 + n])
            )
    late = pltpu.make_async_copy(lift_ref, lift_out, sems.at[3 + 2 * NB])
    for copy in copies + [late]:
        copy.start()
    for copy in copies[1:3]:
        copy.wait()
    drive = packed(couple[...], wave[...])
    for copy in copies[:1] + copies[3:]:
        copy.wait()
    ys = []
    for i in range(2):
        at = slice(i * BLK, (i + 1) * BLK)
        both = []
        for k in range(NB):
            pair = blocks[i * NB + k]
            both.append(jnp.concatenate([pair[0], pair[1]], axis=1))
            both.append(jnp.concatenate([twist(pair[0]), twist(pair[1])], axis=1))
        ys.append(front_rows(held[at, :], jnp.concatenate(both, axis=0)))
        cols_ref[at, :] = tail_columns(held[at, :], patt_ref, BROWS - 2 + i)
    y = jnp.concatenate(ys, axis=0)
    y0, y1 = y[:, :BND], y[:, BND:]
    drive = drive - y0
    c = lax.axis_index(C)
    for out, which in ((keep_ref, c), (send_ref, 1 - c)):
        out[:BND] = pair_of(half_of(drive, which), half_of(y0, which))
        later = half_of(y1, 1 - which)
        out[BND:] = pair_of(later, later)
    late.wait()


def lift_kernel(beat, own_tree, far_tree, keep_ref, came_ref, own_lift, far_lift, *refs):
    copies = ()
    if beat == 0:
        *refs, tree_here, sem = refs
        copies = (pltpu.make_async_copy(own_tree, tree_here, sem),)
        for copy in copies:
            copy.start()
        own_tree = tree_here
    acc = refs[-1]
    outs = refs[-1 - NX : -1]
    x = lax.axis_index(X)
    acc[...] = jnp.zeros_like(acc)
    if beat == 0:
        drives = keep_ref[:BND], came_ref[:BND]
    else:
        own_couple, far_couple, wave_ref = refs[:3]
        wave = wave_ref[...]
        drives = (
            applied(own_couple[...], to_first(wave)) - keep_ref[BND:],
            applied(far_couple[...], wave) - came_ref[BND:],
        )
    parts = [applied(own_lift[...], drives[0]), applied(far_lift[...], drives[1])]
    for copy in copies:
        copy.wait()
    first = is_first(parts[0][:BND]).astype(jnp.int32)
    for tree, part in zip((own_tree, far_tree), parts):
        for p in range(P_SIZE):
            block = tree[p]
            owner = (block % 8) // 2
            slot = lax.rem(owner - x + NX, NX) * 2 + block % 2
            term = part[p * BND : (p + 1) * BND]
            acc[slot] += jnp.where(first == 1 - block // 8, term, 0.0)

    at = 0
    for out in outs:
        for i in range(out.shape[0] // BND):
            out[i * BND : (i + 1) * BND] = acc[at]
            at += 1


def sep_kernel(*refs):
    pieces, (own_ref, far_ref, out_ref) = refs[:-3], refs[-3:]
    x = lax.axis_index(X)
    total = None
    for slot in range(NX):
        owner = lax.rem(x - slot + NX, NX)
        piece = pieces[slot][...]

        def columns(ref, base):
            return jnp.concatenate(
                [
                    ref[:, pl.ds(pl.multiple_of(base + at + owner * QUARTER, QUARTER), QUARTER)]
                    for at in (0, HALF)
                ],
                axis=1,
            )

        rows = jnp.concatenate(
            [columns(ref, base) for ref in (own_ref, far_ref) for base in (0, SEP)], axis=0
        )
        field = jnp.concatenate([piece, to_first(piece)], axis=0)
        part = mm(rows_split(rows), wide(field))
        total = part if total is None else total + part
    total = narrow(total)
    own = total[:BND] + twist(total[BND : 2 * BND])
    far = total[2 * BND : 3 * BND] + twist(total[3 * BND :])
    out_ref[...] = jnp.where(is_first(own), own, far)


def spread_kernel(beat, own_tree, far_tree, own_mat, far_mat, *refs):
    pieces, sol = refs[: 2 * NX], refs[-1]
    x, z, c = lax.axis_index(X), lax.axis_index(Z), lax.axis_index(C)
    for i, piece in enumerate(pieces):
        sol[i] = piece[...]
    zs = []
    for tree, mat in ((own_tree, own_mat), (far_tree, far_mat)):
        both = []
        for p in range(P_SIZE):
            block = tree[p]
            side = lax.rem((block // 2) % 2 + z, 2)
            slot = lax.rem(x - block // 4 + NX, NX)
            field = sol[side * NX + slot]
            field = jnp.where(block % 2 == c, field, to_first(field))
            both += [field, twist(field)]
        zs.append(narrow(mm(rows_split(mat[...]), wide(jnp.concatenate(both, axis=0)))))
    first = is_first(zs[0])
    if beat:
        refs[-2][:BND] = refs[2 * NX][...]
        refs[-2][BND:] = jnp.where(first, zs[0], zs[1])
        return
    keep_ref, came_ref, own_cols, far_cols, z_ref, out_ref = refs[2 * NX : -1]
    z_ref[...] = jnp.where(first, zs[0], zs[1])
    outs = []
    for held, cols, value in zip((keep_ref, came_ref), (own_cols, far_cols), zs):
        moved = narrow(mm(rows_split(cols[...]), wide(tail_field(value))))
        outs.append(held[:BND] - moved)
    out_ref[...] = jnp.where(first, to_first(outs[0]), outs[1])


STEPS = 2
STEP_ROWS = LEAF // STEPS
GROUP = 2


def bulk_kernel(step, patt_ref, src_ref, g_ref, first_ref, second_ref, cols_ref):
    def take(block):
        at = pl.ds(pl.multiple_of(block * BLK, BLK), BLK)
        return src_ref[0, 0, at, :], src_ref[1, 0, at, :]

    def some(n, carry):
        for i in range(GROUP):
            local = n * GROUP + i
            at = pl.ds(pl.multiple_of(local * BLK, BLK), BLK)
            low = pl.ds(pl.multiple_of(STEP_ROWS + local * BLK, BLK), BLK)
            row = step * (STEP_ROWS // BLK) + local
            g = g_ref[at, :]
            y = front_rows(g, gathered(patt_ref, row, take))
            first_ref[at, :] = y[:, :BND]
            second_ref[at, :] = y[:, BND:]
            cols_ref[at, :], cols_ref[low, :] = split(tail_columns(g, patt_ref, row))
        return carry

    lax.fori_loop(0, STEP_ROWS // BLK // GROUP, some, 0)


def field_kernel(own_ref, came_ref, *refs):
    y_refs, col_refs = refs[: 2 * STEPS], refs[2 * STEPS : 3 * STEPS]
    out_ref, buffer, sems = refs[3 * STEPS :]
    copies = []
    for beat in range(BEATS):
        own = own_ref[beat * BND : (beat + 1) * BND]
        came = came_ref[beat * BND : (beat + 1) * BND]
        first = is_first(own)
        z = jnp.where(
            lax.axis_index(C) == beat,
            jnp.where(first, own, came),
            jnp.where(first, to_first(came), to_second(own)),
        )
        tail = cols_split(tail_field(z))
        for i in range(STEPS):
            buffer[beat, i] = y_refs[2 * i + beat][...] - product(col_refs[i][...], tail)
            copy = pltpu.make_async_copy(
                buffer.at[beat, i],
                out_ref.at[beat, pl.ds(i * STEP_ROWS, STEP_ROWS), :],
                sems.at[beat, i],
            )
            copy.start()
            copies.append(copy)
    for copy in copies:
        copy.wait()


VM = pl.BlockSpec(memory_space=pltpu.VMEM)
SM = pl.BlockSpec(memory_space=pltpu.SMEM)


def shape(*dims):
    return jax.ShapeDtypeStruct(dims, F32)


ROOM = pltpu.CompilerParams(vmem_limit_bytes=12 << 20)


def cost(flops, size):
    return pl.CostEstimate(flops=flops, bytes_accessed=size, transcendentals=0)


def shifted(value, axis, distance):
    size = lax.axis_size(axis)
    return lax.ppermute(value, axis, [(i, (i + distance) % size) for i in range(size)])


def swapped(value, axis):
    return shifted(value, axis, 1)


HB = pl.BlockSpec(memory_space=pltpu.HBM)


def in_hbm(value):
    return pltpu.with_memory_space_constraint(value, pltpu.HBM)


def around(pieces):
    got = [pieces[0]] + [None] * (NX - 1)
    for d in (2, 1, 3):
        got[d] = shifted(pieces[d], X, d)
    return got


def sweep(sources, front_inv, pattern, tree, lift, spread, couple, sep_inv, inflow):
    gmat, own_tree, patt = front_inv[0], tree[0, 0], pattern[0].T
    own_spread, kmat, own_sep = spread[0], couple[0], sep_inv[0]
    whole = lambda *dims: pl.BlockSpec(dims, lambda *i: (0,) * len(dims))
    block, double = shape(BND, BND), shape(2 * BND, BND)

    far_tree = swapped(own_tree, C)
    far_lift = swapped(lift[0], C)
    far_sep = swapped(own_sep, C)
    far_spread = swapped(own_spread, C)
    far_couple = swapped(kmat, C)

    keep, send, own_cols, own_lift = pl.pallas_call(
        start_kernel,
        in_specs=[SM, HB, HB, HB, HB, HB],
        out_specs=[VM, VM, VM, VM],
        out_shape=[double, double, shape(BND, 2 * BND), shape(P_SIZE * BND, 2 * BND)],
        scratch_shapes=[
            pltpu.VMEM((2 * NB, 2, BLK, BND), F32),
            pltpu.VMEM((BND, NB * 2 * BLK), F32),
            pltpu.VMEM((BND, 2 * BND), F32),
            pltpu.VMEM((BND, BND), F32),
            pltpu.SemaphoreType.DMA((4 + 2 * NB,)),
        ],
        compiler_params=ROOM,
        cost_estimate=cost(2 * 128 * 512 * 256 * 6, 1 << 21),
        name="start",
    )(patt, *[in_hbm(a) for a in (sources, front_inv, couple, inflow, lift[0])])
    came = swapped(send, C)
    far_cols = swapped(own_cols, C)

    ys, cols = [], []
    for step in range(STEPS):
        y0, y1, col = pl.pallas_call(
            functools.partial(bulk_kernel, step),
            grid=(1,),
            in_specs=[
                SM,
                whole(2, 1, LEAF, BND),
                pl.BlockSpec((STEP_ROWS, NB * 2 * BLK), lambda i, step=step: (step, 0)),
            ],
            out_specs=[
                whole(STEP_ROWS, BND),
                whole(STEP_ROWS, BND),
                whole(2 * STEP_ROWS, 2 * BND),
            ],
            out_shape=[
                shape(STEP_ROWS, BND),
                shape(STEP_ROWS, BND),
                jax.ShapeDtypeStruct((2 * STEP_ROWS, 2 * BND), BF16),
            ],
            compiler_params=ROOM,
            cost_estimate=cost(2 * 512 * 512 * 256 * 6, 3 << 20),
        )(patt, sources, gmat)
        ys.append((y0, y1))
        cols.append(col)

    for beat in range(BEATS):
        extra = ()
        if beat:
            devices = lax.axis_size("slab")
            route = [(2 * i + c, 2 * i + 3 - c) for i in range(devices - 1) for c in range(2)]
            incoming = lax.ppermute(outgoing, ("slab", C), route)
            extra = (kmat, far_couple, incoming)
        fetched = [
            pltpu.SMEM((P_SIZE,), jnp.int32),
            pltpu.SemaphoreType.DMA,
        ]
        fetched = [] if beat else fetched
        pieces = pl.pallas_call(
            functools.partial(lift_kernel, beat),
            in_specs=[SM if beat else HB, SM] + [VM] * (4 + len(extra)),
            out_specs=[VM] * NX,
            out_shape=[double] * NX,
            scratch_shapes=[pltpu.VMEM((2 * NX, BND, BND), F32)] + fetched,
            compiler_params=ROOM,
            cost_estimate=cost(2 * 512 * 256 * 128 * 4, 3 << 19),
        )(
            own_tree if beat else in_hbm(own_tree),
            far_tree,
            keep,
            came,
            own_lift,
            far_lift,
            *extra,
        )
        got = around(pieces)
        near = (pieces[0] + got[1]) + (got[2] + got[3])
        mine = near + swapped(near, Z)
        held = around([mine] * NX)
        sol = pl.pallas_call(
            sep_kernel,
            in_specs=[VM] * (NX + 2),
            out_specs=VM,
            out_shape=block,
            compiler_params=ROOM,
            cost_estimate=cost(2 * 256 * 2048 * 128 * 4, 5 << 20),
        )(*held, own_sep, far_sep)
        other = swapped(sol, Z)
        held = around([sol] * NX) + around([other] * NX)
        extra = (zvals,) if beat else (keep, came, own_cols, far_cols)
        answer = pl.pallas_call(
            functools.partial(spread_kernel, beat),
            in_specs=[SM, SM] + [VM] * (2 * NX + 2 + len(extra)),
            out_specs=[VM] * (2 - beat),
            out_shape=[double] if beat else [block] * 2,
            scratch_shapes=[pltpu.VMEM((2 * NX, BND, BND), F32)],
            compiler_params=ROOM,
            cost_estimate=cost(2 * 128 * 1024 * 128 * 4, 3 << 19),
        )(own_tree, far_tree, own_spread, far_spread, *held, *extra)
        zvals, outgoing = answer[0], answer[-1]
    zcame = swapped(zvals, C)
    result = pl.pallas_call(
        field_kernel,
        in_specs=[VM] * (2 + 3 * STEPS),
        out_specs=pl.BlockSpec(memory_space=pl.ANY),
        out_shape=shape(BEATS, LEAF, BND),
        scratch_shapes=[
            pltpu.VMEM((BEATS, STEPS, STEP_ROWS, BND), F32),
            pltpu.SemaphoreType.DMA((BEATS, STEPS)),
        ],
        compiler_params=ROOM,
        cost_estimate=cost(2 * 1024 * 256 * 256 * 4, 3 << 20),
        name="field",
    )(zvals, zcame, *ys[0], *ys[1], *cols)
    return result[:, None]


def solution(mesh):
    torus = Mesh(
        mesh.devices.reshape(mesh.shape["slab"], 4, 2, 2), ("slab", "front_0", "front_1", "front_2")
    )
    in_specs = (
        P(None, "slab", FRONT, None),
        P("slab", FRONT, None),
        P("slab", FRONT, None),
        P("slab", FRONT, None),
        P("slab", FRONT, None),
        P("slab", FRONT, None),
        P("slab", FRONT, None),
        P("slab", FRONT, None),
        P("slab", FRONT, None),
    )
    out_specs = P(None, "slab", FRONT, None)
    return jax.shard_map(sweep, mesh=torus, in_specs=in_specs, out_specs=out_specs, check_vma=False)
```

```python
import functools

import jax
import jax.numpy as jnp
from jax import lax
from jax.experimental import pallas as pl
from jax.experimental.pallas import tpu as pltpu
from jax.sharding import Mesh
from jax.sharding import PartitionSpec as P

BEATS = 2
LEAF = 1024
SEP = 2048
BLK = 64
NB = 4
BND = 128
P_SIZE = 4
BROWS = LEAF // BLK
FRONT = ("front_0", "front_1", "front_2")
X, Z, C = FRONT
NX = 4
HALF = SEP // 2
QUARTER = HALF // NX
F32 = jnp.float32
BF16 = jnp.bfloat16


def twist(field):
    half = field.shape[-1] // 2
    lane = lax.broadcasted_iota(jnp.int32, field.shape, len(field.shape) - 1)
    turned = pltpu.roll(field, half, len(field.shape) - 1)
    return jnp.where(lane < half, -turned, turned)


def split(a):
    high = a.astype(BF16)
    low = (a - high.astype(F32)).astype(BF16)
    return high, low


def mm(a, b):
    return jnp.dot(a, b, preferred_element_type=F32)


def rows_split(a):
    return jnp.concatenate(split(a), axis=0)


def cols_split(b):
    return jnp.concatenate(split(b), axis=1)


def product(stacked, paired):
    rows, cols = stacked.shape[0] // 2, paired.shape[1] // 2
    full = mm(stacked, paired)
    return full[:rows, :cols] + (full[:rows, cols:] + full[rows:, :cols])


def packed(matrix, field):
    both = jnp.concatenate([field, twist(field)], axis=0)
    return product(rows_split(matrix), cols_split(both))


QUAD = 32


def is_first(field):
    lane = lax.broadcasted_iota(jnp.int32, field.shape, 1)
    return (lane // QUAD) % 2 == 0


def to_second(field):
    return pltpu.roll(field, QUAD, 1)


def to_first(field):
    return pltpu.roll(field, field.shape[1] - QUAD, 1)


def pair_of(first, second):
    return jnp.where(is_first(first), first, to_second(second))


def half_of(field, c):
    return jnp.where(c == 0, field, to_first(field))


def wide(field):
    high = field.astype(BF16).astype(F32)
    return pair_of(high, field - high).astype(BF16)


def narrow(full):
    rows = full.shape[0] // 2
    total = full[:rows] + full[rows:]
    return total + jnp.where(is_first(total), to_first(total), to_second(total))


def applied(matrix, field):
    both = jnp.concatenate([field, twist(field)], axis=0)
    return narrow(mm(rows_split(matrix), wide(both)))


def front_rows(g, field):
    gh, gl = split(g)
    fh, fl = split(field)
    rows = g.shape[0]
    first = mm(jnp.concatenate([gh, gl], axis=0), fh)
    return first[:rows] + (first[rows:] + mm(gh, fl))


def gathered(patt_ref, row, take):
    both = []
    for k in range(NB):
        a, b = take(patt_ref[k, row])
        both.append(jnp.concatenate([a, b], axis=1))
        both.append(jnp.concatenate([twist(a), twist(b)], axis=1))
    return jnp.concatenate(both, axis=0)


def tail_columns(g, patt_ref, row):
    parts = []
    for block in (BROWS - 2, BROWS - 1):
        total = jnp.zeros((BLK, 2 * BLK), F32)
        for k in range(NB):
            held = (patt_ref[k, row] == block).astype(F32)
            total = total + held * g[:, k * 2 * BLK : (k + 1) * 2 * BLK]
        parts.append(total)
    return jnp.concatenate(parts, axis=1)


def tail_field(z):
    tz = twist(z)
    return jnp.concatenate([z[:BLK], tz[:BLK], z[BLK:], tz[BLK:]], axis=0)


def start_kernel(
    patt_ref, src_ref, g_ref, couple_ref, wave_ref, lift_ref, keep_ref, send_ref, cols_ref, lift_out, blocks, held, couple, wave, sems
):
    copies = [
        pltpu.make_async_copy(g_ref.at[0, pl.ds(LEAF - BND, BND), :], held, sems.at[0]),
        pltpu.make_async_copy(couple_ref.at[0], couple, sems.at[1]),
        pltpu.make_async_copy(wave_ref.at[0], wave, sems.at[2]),
    ]
    for i in range(2):
        for k in range(NB):
            at = pl.ds(pl.multiple_of(patt_ref[k, BROWS - 2 + i] * BLK, BLK), BLK)
            n = i * NB + k
            copies.append(
                pltpu.make_async_copy(src_ref.at[:, 0, at, :], blocks.at[n], sems.at[3 + n])
            )
    late = pltpu.make_async_copy(lift_ref, lift_out, sems.at[3 + 2 * NB])
    for copy in copies + [late]:
        copy.start()
    for copy in copies[1:3]:
        copy.wait()
    drive = packed(couple[...], wave[...])
    for copy in copies[:1] + copies[3:]:
        copy.wait()
    ys = []
    for i in range(2):
        at = slice(i * BLK, (i + 1) * BLK)
        both = []
        for k in range(NB):
            pair = blocks[i * NB + k]
            both.append(jnp.concatenate([pair[0], pair[1]], axis=1))
            both.append(jnp.concatenate([twist(pair[0]), twist(pair[1])], axis=1))
        ys.append(front_rows(held[at, :], jnp.concatenate(both, axis=0)))
        cols_ref[at, :] = tail_columns(held[at, :], patt_ref, BROWS - 2 + i)
    y = jnp.concatenate(ys, axis=0)
    y0, y1 = y[:, :BND], y[:, BND:]
    drive = drive - y0
    c = lax.axis_index(C)
    for out, which in ((keep_ref, c), (send_ref, 1 - c)):
        out[:BND] = pair_of(half_of(drive, which), half_of(y0, which))
        later = half_of(y1, which)
        out[BND:] = pair_of(later, later)
    late.wait()


def lift_kernel(beat, own_tree, far_tree, keep_ref, came_ref, own_lift, far_lift, *refs):
    copies = ()
    if beat == 0:
        *refs, tree_here, sem = refs
        copies = (pltpu.make_async_copy(own_tree, tree_here, sem),)
        for copy in copies:
            copy.start()
        own_tree = tree_here
    acc = refs[-1]
    outs = refs[-1 - NX : -1]
    x = lax.axis_index(X)
    acc[...] = jnp.zeros_like(acc)
    if beat == 0:
        drives = keep_ref[:BND], came_ref[:BND]
    else:
        own_couple, far_couple, wave_ref = refs[:3]
        wave = wave_ref[...]
        drives = (
            applied(own_couple[...], wave) - keep_ref[BND:],
            applied(far_couple[...], to_first(wave)) - came_ref[BND:],
        )
    parts = [applied(own_lift[...], drives[0]), applied(far_lift[...], drives[1])]
    for copy in copies:
        copy.wait()
    first = is_first(parts[0][:BND]).astype(jnp.int32)
    for tree, part in zip((own_tree, far_tree), parts):
        for p in range(P_SIZE):
            block = tree[p]
            owner = (block % 8) // 2
            slot = lax.rem(owner - x + NX, NX) * 2 + block % 2
            term = part[p * BND : (p + 1) * BND]
            acc[slot] += jnp.where(first == 1 - block // 8, term, 0.0)

    at = 0
    for out in outs:
        for i in range(out.shape[0] // BND):
            out[i * BND : (i + 1) * BND] = acc[at]
            at += 1


def sep_kernel(*refs):
    pieces, (own_ref, far_ref, out_ref) = refs[:-3], refs[-3:]
    x = lax.axis_index(X)
    total = None
    for slot in range(NX):
        owner = lax.rem(x - slot + NX, NX)
        piece = pieces[slot][...]

        def columns(ref, base):
            return jnp.concatenate(
                [
                    ref[:, pl.ds(pl.multiple_of(base + at + owner * QUARTER, QUARTER), QUARTER)]
                    for at in (0, HALF)
                ],
                axis=1,
            )

        rows = jnp.concatenate(
            [columns(ref, base) for ref in (own_ref, far_ref) for base in (0, SEP)], axis=0
        )
        field = jnp.concatenate([piece, to_first(piece)], axis=0)
        part = mm(rows_split(rows), wide(field))
        total = part if total is None else total + part
    total = narrow(total)
    own = total[:BND] + twist(total[BND : 2 * BND])
    far = total[2 * BND : 3 * BND] + twist(total[3 * BND :])
    out_ref[...] = jnp.where(is_first(own), own, far)


def spread_kernel(beat, own_tree, far_tree, own_mat, far_mat, *refs):
    pieces, sol = refs[: 2 * NX], refs[-1]
    x, z, c = lax.axis_index(X), lax.axis_index(Z), lax.axis_index(C)
    for i, piece in enumerate(pieces):
        sol[i] = piece[...]
    zs = []
    for tree, mat in ((own_tree, own_mat), (far_tree, far_mat)):
        both = []
        for p in range(P_SIZE):
            block = tree[p]
            side = lax.rem((block // 2) % 2 + z, 2)
            slot = lax.rem(x - block // 4 + NX, NX)
            field = sol[side * NX + slot]
            field = jnp.where(block % 2 == c, field, to_first(field))
            both += [field, twist(field)]
        zs.append(narrow(mm(rows_split(mat[...]), wide(jnp.concatenate(both, axis=0)))))
    first = is_first(zs[0])
    if beat:
        refs[-2][:BND] = refs[2 * NX][...]
        refs[-2][BND:] = jnp.where(first, zs[0], zs[1])
        return
    keep_ref, came_ref, own_cols, far_cols, z_ref, out_ref = refs[2 * NX : -1]
    z_ref[...] = jnp.where(first, zs[0], zs[1])
    outs = []
    for held, cols, value in zip((keep_ref, came_ref), (own_cols, far_cols), zs):
        moved = narrow(mm(rows_split(cols[...]), wide(tail_field(value))))
        outs.append(held[:BND] - moved)
    out_ref[...] = jnp.where(first, to_first(outs[0]), outs[1])


STEPS = 2
STEP_ROWS = LEAF // STEPS
GROUP = 2


def bulk_kernel(step, patt_ref, src_ref, g_ref, first_ref, second_ref, cols_ref):
    def take(block):
        at = pl.ds(pl.multiple_of(block * BLK, BLK), BLK)
        return src_ref[0, 0, at, :], src_ref[1, 0, at, :]

    def some(n, carry):
        for i in range(GROUP):
            local = n * GROUP + i
            at = pl.ds(pl.multiple_of(local * BLK, BLK), BLK)
            low = pl.ds(pl.multiple_of(STEP_ROWS + local * BLK, BLK), BLK)
            row = step * (STEP_ROWS // BLK) + local
            g = g_ref[at, :]
            y = front_rows(g, gathered(patt_ref, row, take))
            first_ref[at, :] = y[:, :BND]
            second_ref[at, :] = y[:, BND:]
            cols_ref[at, :], cols_ref[low, :] = split(tail_columns(g, patt_ref, row))
        return carry

    lax.fori_loop(0, STEP_ROWS // BLK // GROUP, some, 0)


def field_kernel(own_ref, came_ref, *refs):
    y_refs, col_refs = refs[: 2 * STEPS], refs[2 * STEPS : 3 * STEPS]
    out_ref, buffer, sems = refs[3 * STEPS :]
    copies = []
    for beat in range(BEATS):
        own = own_ref[beat * BND : (beat + 1) * BND]
        came = came_ref[beat * BND : (beat + 1) * BND]
        first = is_first(own)
        z = jnp.where(
            lax.axis_index(C) == 0,
            jnp.where(first, own, came),
            jnp.where(first, to_first(came), to_second(own)),
        )
        tail = cols_split(tail_field(z))
        for i in range(STEPS):
            buffer[beat, i] = y_refs[2 * i + beat][...] - product(col_refs[i][...], tail)
            copy = pltpu.make_async_copy(
                buffer.at[beat, i],
                out_ref.at[beat, pl.ds(i * STEP_ROWS, STEP_ROWS), :],
                sems.at[beat, i],
            )
            copy.start()
            copies.append(copy)
    for copy in copies:
        copy.wait()


VM = pl.BlockSpec(memory_space=pltpu.VMEM)
SM = pl.BlockSpec(memory_space=pltpu.SMEM)


def shape(*dims):
    return jax.ShapeDtypeStruct(dims, F32)


ROOM = pltpu.CompilerParams(vmem_limit_bytes=12 << 20)


def cost(flops, size):
    return pl.CostEstimate(flops=flops, bytes_accessed=size, transcendentals=0)


def shifted(value, axis, distance):
    size = lax.axis_size(axis)
    return lax.ppermute(value, axis, [(i, (i + distance) % size) for i in range(size)])


def swapped(value, axis):
    return shifted(value, axis, 1)


HB = pl.BlockSpec(memory_space=pltpu.HBM)


def in_hbm(value):
    return pltpu.with_memory_space_constraint(value, pltpu.HBM)


def around(pieces):
    got = [pieces[0]] + [None] * (NX - 1)
    for d in (2, 1, 3):
        got[d] = shifted(pieces[d], X, d)
    return got


def sweep(sources, front_inv, pattern, tree, lift, spread, couple, sep_inv, inflow):
    gmat, own_tree, patt = front_inv[0], tree[0, 0], pattern[0].T
    own_spread, kmat, own_sep = spread[0], couple[0], sep_inv[0]
    whole = lambda *dims: pl.BlockSpec(dims, lambda *i: (0,) * len(dims))
    block, double = shape(BND, BND), shape(2 * BND, BND)

    far_tree = swapped(own_tree, C)
    far_lift = swapped(lift[0], C)
    far_sep = swapped(in_hbm(own_sep), C)
    far_spread = swapped(own_spread, C)
    far_couple = swapped(kmat, C)

    keep, send, own_cols, own_lift = pl.pallas_call(
        start_kernel,
        in_specs=[SM, HB, HB, HB, HB, HB],
        out_specs=[VM, VM, VM, VM],
        out_shape=[double, double, shape(BND, 2 * BND), shape(P_SIZE * BND, 2 * BND)],
        scratch_shapes=[
            pltpu.VMEM((2 * NB, 2, BLK, BND), F32),
            pltpu.VMEM((BND, NB * 2 * BLK), F32),
            pltpu.VMEM((BND, 2 * BND), F32),
            pltpu.VMEM((BND, BND), F32),
            pltpu.SemaphoreType.DMA((4 + 2 * NB,)),
        ],
        compiler_params=ROOM,
        cost_estimate=cost(2 * 128 * 512 * 256 * 6, 1 << 21),
        name="start",
    )(patt, *[in_hbm(a) for a in (sources, front_inv, couple, inflow, lift[0])])
    came = swapped(send, C)
    far_cols = swapped(own_cols, C)

    ys, cols = [], []
    for step in range(STEPS):
        y0, y1, col = pl.pallas_call(
            functools.partial(bulk_kernel, step),
            grid=(1,),
            in_specs=[
                SM,
                whole(2, 1, LEAF, BND),
                pl.BlockSpec((STEP_ROWS, NB * 2 * BLK), lambda i, step=step: (step, 0)),
            ],
            out_specs=[
                whole(STEP_ROWS, BND),
                whole(STEP_ROWS, BND),
                whole(2 * STEP_ROWS, 2 * BND),
            ],
            out_shape=[
                shape(STEP_ROWS, BND),
                shape(STEP_ROWS, BND),
                jax.ShapeDtypeStruct((2 * STEP_ROWS, 2 * BND), BF16),
            ],
            compiler_params=ROOM,
            cost_estimate=cost(2 * 512 * 512 * 256 * 6, 3 << 20),
        )(patt, sources, gmat)
        ys.append((y0, y1))
        cols.append(col)

    for beat in range(BEATS):
        extra = ()
        if beat:
            devices = lax.axis_size("slab")
            incoming = lax.ppermute(outgoing, "slab", [(i, i + 1) for i in range(devices - 1)])
            extra = (kmat, far_couple, incoming)
        fetched = [
            pltpu.SMEM((P_SIZE,), jnp.int32),
            pltpu.SemaphoreType.DMA,
        ]
        fetched = [] if beat else fetched
        pieces = pl.pallas_call(
            functools.partial(lift_kernel, beat),
            in_specs=[SM if beat else HB, SM] + [VM] * (4 + len(extra)),
            out_specs=[VM] * NX,
            out_shape=[double] * NX,
            scratch_shapes=[pltpu.VMEM((2 * NX, BND, BND), F32)] + fetched,
            compiler_params=ROOM,
            cost_estimate=cost(2 * 512 * 256 * 128 * 4, 3 << 19),
        )(
            own_tree if beat else in_hbm(own_tree),
            far_tree,
            keep,
            came,
            own_lift,
            far_lift,
            *extra,
        )
        got = around(pieces)
        near = (pieces[0] + got[1]) + (got[2] + got[3])
        mine = near + swapped(near, Z)
        held = around([mine] * NX)
        sol = pl.pallas_call(
            sep_kernel,
            in_specs=[VM] * (NX + 2),
            out_specs=VM,
            out_shape=block,
            compiler_params=ROOM,
            cost_estimate=cost(2 * 256 * 2048 * 128 * 4, 5 << 20),
        )(*held, own_sep, far_sep)
        other = swapped(sol, Z)
        held = around([sol] * NX) + around([other] * NX)
        extra = (zvals,) if beat else (keep, came, own_cols, far_cols)
        answer = pl.pallas_call(
            functools.partial(spread_kernel, beat),
            in_specs=[SM, SM] + [VM] * (2 * NX + 2 + len(extra)),
            out_specs=[VM] * (2 - beat),
            out_shape=[double] if beat else [block] * 2,
            scratch_shapes=[pltpu.VMEM((2 * NX, BND, BND), F32)],
            compiler_params=ROOM,
            cost_estimate=cost(2 * 128 * 1024 * 128 * 4, 3 << 19),
        )(own_tree, far_tree, own_spread, far_spread, *held, *extra)
        zvals, outgoing = answer[0], answer[-1]
    zcame = swapped(zvals, C)
    result = pl.pallas_call(
        field_kernel,
        in_specs=[VM] * (2 + 3 * STEPS),
        out_specs=pl.BlockSpec(memory_space=pl.ANY),
        out_shape=shape(BEATS, LEAF, BND),
        scratch_shapes=[
            pltpu.VMEM((BEATS, STEPS, STEP_ROWS, BND), F32),
            pltpu.SemaphoreType.DMA((BEATS, STEPS)),
        ],
        compiler_params=ROOM,
        cost_estimate=cost(2 * 1024 * 256 * 256 * 4, 3 << 20),
        name="field",
    )(zvals, zcame, *ys[0], *ys[1], *cols)
    return result[:, None]


def solution(mesh):
    torus = Mesh(
        mesh.devices.reshape(mesh.shape["slab"], 4, 2, 2), ("slab", "front_0", "front_1", "front_2")
    )
    in_specs = (
        P(None, "slab", FRONT, None),
        P("slab", FRONT, None),
        P("slab", FRONT, None),
        P("slab", FRONT, None),
        P("slab", FRONT, None),
        P("slab", FRONT, None),
        P("slab", FRONT, None),
        P("slab", FRONT, None),
        P("slab", FRONT, None),
    )
    out_specs = P(None, "slab", FRONT, None)
    return jax.shard_map(sweep, mesh=torus, in_specs=in_specs, out_specs=out_specs, check_vma=False)
```
